512 devices in a mesh: range: 64 (over x, z, core), grp: 8 (over y).
Axes of the slice: x: 4, y: 8, z: 8, core: 2. Of those that a mesh axis runs over, the one named last changes fastest.
Arguments:
- amplitudes: float32 [512, 128, 16, 128], P(('range', 'grp')), may hold values from -6 to 6
- integrals: float32 [65536, 1024], P(('range', 'grp')), may hold values from -0.046875 to 0.046875
- occupancy: int32 [512, 128], P(('range', 'grp')), may hold values from 0 to 511, as said below
- tile_place: int32 [512], replicated, may hold values from 0 to 511, as said below
Outputs:
- ladder: float32 [8192, 1024], P(('range', 'grp'))
The draws below stay inside these ranges and needn't reach their ends.
Inputs may be any that keep to these rules, and one draw needn't show every extreme that they name: `occupancy`: each block row lists 128 distinct contracted tiles. At most 4 tiles of one block row have tile_place // 8 equal to the same value, and in every draw one such value is reached by exactly 4 tiles in every block row. `tile_place`: a permutation of 0 to 511; the range index tile_place[k] // 8 owns tile k.
All inputs are finite; a program needn't handle non-finite values.
Results may differ from the reference program's by a relative error of at most 0.0003.
Values sent between devices are 32-bit elements; how exact they have to be, the bound alone decides.
No kernel may reach another device: no remote copies, remote signals or barrier semaphores. Data moves between devices by JAX's collectives and lax.ppermute only.
A program may use at most 64 MiB of HBM per device.

```python
import jax
import jax.numpy as jnp
from jax import lax

TW = 128
TROW = 16
OUT = 1024
KT_DEV = 8
CAP = 4
KT = 512
OCC = 128
NB = 512
N_RANGE = 64


def build_layout(key):
    tile_place = jax.random.permutation(jax.random.fold_in(key, 11), KT).astype(jnp.int32)
    hot_owner = jax.random.randint(jax.random.fold_in(key, 12), (), 0, N_RANGE).astype(jnp.int32)
    row_keys = jax.random.split(jax.random.fold_in(key, 13), NB)
    owner_order = jax.vmap(lambda k: jax.random.permutation(k, N_RANGE))(row_keys).astype(jnp.int32)
    base_count = OCC // N_RANGE
    spread = CAP - base_count
    shifts = jax.random.randint(jax.random.fold_in(key, 14), (NB, N_RANGE // 2), -spread, spread + 1).astype(jnp.int32)
    count_pos = jnp.stack([base_count + shifts, base_count - shifts], axis=-1).reshape(NB, N_RANGE)
    positions = jnp.arange(N_RANGE, dtype=jnp.int32)[None, :]
    hot_pos = jnp.argmax((owner_order == hot_owner).astype(jnp.int32), axis=1).astype(jnp.int32)[:, None]
    partner_pos = jnp.bitwise_xor(hot_pos, 1)
    count_pos = jnp.where(positions == hot_pos, base_count + spread, jnp.where(positions == partner_pos, base_count - spread, count_pos))
    inverse_order = jnp.argsort(owner_order, axis=1).astype(jnp.int32)
    counts = jnp.take_along_axis(count_pos, inverse_order, axis=1)
    slot_iota = jnp.arange(KT_DEV, dtype=jnp.int32)[None, None, :]
    slot_scores = jax.random.randint(jax.random.fold_in(key, 15), (NB, N_RANGE, KT_DEV), 0, 2 ** 20).astype(jnp.int32) * KT_DEV + slot_iota
    slot_rank = jnp.argsort(jnp.argsort(slot_scores, axis=2), axis=2).astype(jnp.int32)
    chosen = (slot_rank < counts[:, :, None]).reshape(NB, N_RANGE * KT_DEV)
    place_iota = jnp.arange(N_RANGE * KT_DEV, dtype=jnp.int32)[None, :]
    order_scores = jax.random.randint(jax.random.fold_in(key, 16), (NB, N_RANGE * KT_DEV), 0, 2 ** 20).astype(jnp.int32) * (N_RANGE * KT_DEV) + place_iota
    order_scores = jnp.where(chosen, order_scores, 2 ** 30 + place_iota)
    places = jnp.argsort(order_scores, axis=1)[:, :OCC].astype(jnp.int32)
    tile_of_place = jnp.argsort(tile_place).astype(jnp.int32)
    occupancy = tile_of_place[places].astype(jnp.int32)
    return (tile_place, occupancy)


def draw_tile_place(key, part):
    return build_layout(key)[0]


def draw_occupancy(key, part):
    return build_layout(key)[1]


def level_of(rng, dims, shards, low, largest):
    loudness, own = 1.0, jax.random.fold_in(rng, 6)
    for dim, blocks in shards:
        draws = jnp.exp(jax.random.uniform(jax.random.fold_in(own, dim), (blocks,), jnp.float32, low / len(shards), largest / len(shards)))
        loudness = loudness * jnp.repeat(draws, dims[dim] // blocks).reshape([-1 if axis == dim else 1 for axis in range(len(dims))])
    return loudness


def noise(rng, dims, scale, reach, cuts=(), kind=jnp.bfloat16):
    entries = scale * jax.random.normal(rng, dims, jnp.float32)
    if cuts:
        entries = entries * level_of(rng, dims, cuts, -0.22, 0.18)
    return jnp.clip(entries, -reach, reach).astype(kind)


def setup_inputs(seed: int = 0) -> dict:
    key_list = jax.random.split(jax.random.key(seed), 5)
    amplitudes = noise(key_list[0], (NB, OCC, TROW, TW), 1.0, 6.0, ((0, 512),), jnp.float32)
    integrals = noise(key_list[1], (KT * TW, OUT), (OCC * TW) ** -0.5, 0.046875, ((0, 512),), jnp.float32)
    occupancy = draw_occupancy(jax.random.fold_in(key_list[4], 71), 0)
    tile_place = draw_tile_place(jax.random.fold_in(key_list[4], 71), 0)
    return {"amplitudes": amplitudes, "integrals": integrals, "occupancy": occupancy, "tile_place": tile_place}


def reference(amplitudes, integrals, occupancy, tile_place):
    blocks_all = integrals.reshape(KT, TW, OUT)

    def one_row(pair):
        amp_row, occ_row = pair
        picked = blocks_all[tile_place[occ_row].astype(jnp.int32)]
        return jnp.einsum("jrt,jtc->rc", amp_row, picked, precision=lax.Precision.HIGHEST)

    ladder = lax.map(one_row, (amplitudes, occupancy))
    return ladder.reshape(NB * TROW, OUT)
```

```python
import jax
import jax.numpy as jnp
import numpy as np
from jax import lax
from jax.experimental import pallas as pl
from jax.experimental.pallas import tpu as pltpu
from jax.sharding import Mesh, PartitionSpec as P

NX, NZ, NC = 4, 8, 2
CAP = 4
RANGE = ("x", "z", "core")
VMEM = pl.BlockSpec(memory_space=pltpu.VMEM)
SMEM = pl.BlockSpec(memory_space=pltpu.SMEM)


def pack_kernel(n_tiles, occ_ref, place_ref, amp_ref, out_ref, slot_ref, count_ref):
    slot_ref[...] = jnp.full(slot_ref.shape, -1, jnp.int32)

    def clear(i, carry):
        count_ref[i] = 0
        return carry

    lax.fori_loop(0, count_ref.shape[0], clear, 0)

    def step(j, carry):
        place = place_ref[occ_ref[j]]
        owner = place // n_tiles
        tile = place % n_tiles
        slot = count_ref[owner]
        count_ref[owner] = slot + 1
        out_ref[owner * CAP + slot] = amp_ref[j]
        slot_ref[owner, pl.ds(slot, 1), :] = jnp.full((1, 128), tile, jnp.int32)
        return carry

    lax.fori_loop(0, occ_ref.shape[0], step, 0, unroll=4)


def pack(occ, place, amp, n_range, n_tiles):
    occ_n, rows, width = amp.shape
    return pl.pallas_call(
        lambda *refs: pack_kernel(n_tiles, *refs),
        out_shape=(
            jax.ShapeDtypeStruct((n_range * CAP, rows, width), jnp.float32),
            jax.ShapeDtypeStruct((n_range, 8, 128), jnp.int32),
        ),
        in_specs=[SMEM, SMEM, VMEM],
        out_specs=(VMEM, VMEM),
        scratch_shapes=[pltpu.SMEM((n_range,), jnp.int32)],
        cost_estimate=pl.CostEstimate(flops=0, bytes_accessed=8 << 20, transcendentals=0),
        name="pack",
    )(occ, place, amp)


def spread_kernel(n_tiles, slot_ref, pos_ref, in_ref, out_ref):
    rows = in_ref.shape[1]
    n_src = slot_ref.shape[0]
    core, grp = pos_ref[0], pos_ref[1]
    out_ref[...] = jnp.zeros_like(out_ref)

    def step(n, carry):
        half = 1 - ((n % NC) ^ core)
        row = pl.multiple_of((half * (n_src // NC) + n // NC) * rows, rows)
        for s in range(CAP):
            tile = slot_ref[n, s]

            @pl.when(tile >= 0)
            def _():
                col = pl.multiple_of(((grp - tile + n_tiles) % n_tiles) * 128, 128)
                out_ref[pl.ds(row, rows), pl.ds(col, 128)] = in_ref[n * CAP + s]

        return carry

    lax.fori_loop(0, n_src, step, 0)


def spread(slots, pos, tiles, n_tiles):
    n_src = slots.shape[0]
    rows, width = tiles.shape[1:]
    return pl.pallas_call(
        lambda *refs: spread_kernel(n_tiles, *refs),
        out_shape=jax.ShapeDtypeStruct((n_src * rows, n_tiles * width), jnp.float32),
        in_specs=[SMEM, SMEM, VMEM],
        out_specs=VMEM,
        cost_estimate=pl.CostEstimate(flops=0, bytes_accessed=8 << 20, transcendentals=0),
        name="spread",
    )(slots, pos, tiles)


def ring(n, step):
    return [(i, (i + step) % n) for i in range(n)]


def gather_panel(block):
    n = lax.axis_size("grp")
    right, left = [block], [block]
    half = block.shape[0] // 2
    for _ in range(n // 2 - 1):
        right.append(lax.ppermute(right[-1], "grp", ring(n, 1)))
        left.append(lax.ppermute(left[-1], "grp", ring(n, -1)))
    far_top = lax.ppermute(right[-1][:half], "grp", ring(n, 1))
    far_bottom = lax.ppermute(left[-1][half:], "grp", ring(n, -1))
    return jnp.concatenate(right + [far_top, far_bottom] + left[:0:-1], axis=0)


def on_device(amplitudes, integrals, occupancy, tile_place):
    n_range = NX * NZ * NC
    n_tiles = tile_place.shape[0] // n_range
    rows, width = amplitudes.shape[2:]
    out_cols = integrals.shape[1]
    panel = gather_panel(integrals)
    sent, slots = pack(occupancy[0], tile_place, amplitudes[0], n_range, n_tiles)
    sent = sent.reshape(n_range, CAP, rows, width)
    tiles = lax.all_to_all(sent, RANGE, 0, 0, tiled=True)
    slots = lax.all_to_all(slots, RANGE, 0, 0, tiled=True)[:, :CAP, 0]
    pos = jnp.stack([lax.axis_index("core"), lax.axis_index("grp")]).astype(jnp.int32)
    left = spread(slots, pos, tiles.reshape(n_range * CAP, rows, width), n_tiles)
    half = left.shape[0] // NC
    other = jnp.dot(left[:half], panel, precision=lax.Precision.HIGH)
    other = lax.ppermute(other, "core", ring(NC, 1))
    mine = jnp.dot(left[half:], panel, precision=lax.Precision.HIGH) + other
    mine = mine.reshape(NX, half // NX, out_cols)
    mine = lax.all_to_all(mine, "x", 0, 0, tiled=True).sum(axis=0)
    mine = mine.reshape(NZ, rows, out_cols)
    return lax.all_to_all(mine, "z", 0, 0, tiled=True).sum(axis=0)


def solution(mesh):
    split = Mesh(mesh.devices.reshape(NX, NZ, NC, -1), RANGE + ("grp",))
    every = RANGE + ("grp",)
    return jax.shard_map(
        on_device,
        mesh=split,
        in_specs=(
            P(every, None, None, None),
            P(every, None),
            P(every, None),
            P(),
        ),
        out_specs=P(every, None),
        check_vma=False,
    )
```

```python
import jax
import jax.numpy as jnp
from jax import lax
from jax.experimental import pallas as pl
from jax.experimental.pallas import tpu as pltpu
from jax.sharding import Mesh, PartitionSpec as P

NX, NZ, NC = 4, 8, 2
CAP = 4
CHIPS = ("x", "z")
EVERY = ("x", "z", "core", "grp")
LANES = 128
HEAD = 8
VMEM = pl.BlockSpec(memory_space=pltpu.VMEM)
SMEM = pl.BlockSpec(memory_space=pltpu.SMEM)
ANY = pl.BlockSpec(memory_space=pl.ANY)


def pack_kernel(per_chip, occ_ref, place_ref, amp_ref, out_ref, count_ref):
    rows = amp_ref.shape[1]
    heading = jnp.full((HEAD, LANES), -1.0, jnp.float32)
    lane = lax.broadcasted_iota(jnp.int32, (HEAD, LANES), 1)

    def clear(i, carry):
        count_ref[i] = 0
        out_ref[i, pl.ds(0, HEAD), :] = heading
        return carry

    lax.fori_loop(0, count_ref.shape[0], clear, 0)

    def step(j, carry):
        place = place_ref[occ_ref[j]]
        chip = place // per_chip
        tile = place % per_chip
        slot = count_ref[chip]
        count_ref[chip] = slot + 1
        out_ref[chip, pl.ds(pl.multiple_of(HEAD + slot * rows, 8), rows), :] = amp_ref[j]
        out_ref[chip, pl.ds(0, HEAD), :] = jnp.where(
            lane == slot, tile.astype(jnp.float32), out_ref[chip, pl.ds(0, HEAD), :]
        )
        return carry

    lax.fori_loop(0, occ_ref.shape[0], step, 0, unroll=4)


def pack(occ, place, amp, chips, per_chip):
    rows, width = amp.shape[1:]
    return pl.pallas_call(
        lambda *refs: pack_kernel(per_chip, *refs),
        out_shape=jax.ShapeDtypeStruct((chips, HEAD + NC * CAP * rows, width), jnp.float32),
        in_specs=[SMEM, SMEM, VMEM],
        out_specs=VMEM,
        scratch_shapes=[pltpu.SMEM((chips,), jnp.int32)],
        cost_estimate=pl.CostEstimate(flops=0, bytes_accessed=8 << 20, transcendentals=0),
        name="pack",
    )(occ, place, amp)


def split(value):
    high = value.astype(jnp.bfloat16)
    return high, (value - high.astype(jnp.float32)).astype(jnp.bfloat16)


def split_kernel(*refs):
    blocks, (high_ref, low_ref) = refs[:-2], refs[-2:]
    at = 0
    for ref in blocks:
        for i in range(0, ref.shape[0], 64):
            high, low = split(ref[i : i + 64, :])
            high_ref[at : at + 64, :] = high
            low_ref[at : at + 64, :] = low
            at += 64


def split_panel(blocks):
    depth = sum(block.shape[0] for block in blocks)
    out = jax.ShapeDtypeStruct((depth, blocks[0].shape[1]), jnp.bfloat16)
    return pl.pallas_call(
        split_kernel,
        out_shape=(out, out),
        in_specs=[VMEM] * len(blocks),
        out_specs=(VMEM, VMEM),
        cost_estimate=pl.CostEstimate(flops=0, bytes_accessed=8 * depth * 1024, transcendentals=0),
        name="split_panel",
    )(*blocks)


def ladder_kernel(pos_ref, got_hbm, high_hbm, low_hbm, out_ref, *scratch):
    got, head, where, v_high, v_low, a_high, a_low, sems = scratch
    chips = got.shape[0]
    per_chip = where.shape[0]
    per_core = per_chip // NC
    rows = out_ref.shape[0] // chips
    core, grp = pos_ref[0], pos_ref[1]
    copies = [
        pltpu.make_async_copy(got_hbm.at[:, pl.ds(0, HEAD), :], head, sems.at[0]),
        pltpu.make_async_copy(got_hbm, got, sems.at[1]),
        pltpu.make_async_copy(high_hbm, v_high, sems.at[2]),
        pltpu.make_async_copy(low_hbm, v_low, sems.at[3]),
    ]
    for copy in copies:
        copy.start()
    a_high[...] = jnp.zeros_like(a_high)
    a_low[...] = jnp.zeros_like(a_low)
    for of_core in range(NC):
        for of_grp in range(per_core):
            where[of_core * per_core + of_grp] = panel_position(core, grp, of_core, of_grp, per_core)
    copies[0].wait()
    copies[1].wait()

    def step(n, carry):
        row = pl.multiple_of(n * rows, rows)
        for s in range(NC * CAP):
            tile = head[n, 0, s].astype(jnp.int32)

            @pl.when(tile >= 0)
            def _():
                col = pl.multiple_of(where[tile] * LANES, LANES)
                high, low = split(got[n, HEAD + s * rows : HEAD + (s + 1) * rows, :])
                a_high[pl.ds(row, rows), pl.ds(col, LANES)] = high
                a_low[pl.ds(row, rows), pl.ds(col, LANES)] = low

        return carry

    lax.fori_loop(0, chips, step, 0)
    copies[2].wait()
    copies[3].wait()
    dot = lambda a, b: jnp.dot(a, b, preferred_element_type=jnp.float32)
    wide = 256

    def columns(i, carry):
        cols = pl.ds(pl.multiple_of(i * wide, wide), wide)
        b_high, b_low = v_high[:, cols], v_low[:, cols]
        out_ref[:, cols] = (
            dot(a_high[...], b_high) + dot(a_high[...], b_low) + dot(a_low[...], b_high)
        )
        return carry

    lax.fori_loop(0, out_ref.shape[1] // wide, columns, 0)


def panel_position(core, grp, of_core, of_grp, n):
    ahead = jnp.where(core == 0, grp - of_grp + n, of_grp - grp + n) % n
    other = jnp.where(core == of_core, 0, 1)
    near = 2 * ahead + other
    swapped = n + 2 * (n - ahead - 1) + 1 - other
    return jnp.where(ahead < n // 2, near, jnp.where(ahead == n // 2, 2 * n - 2 + other, swapped))


def ladder(pos, got, high, low, rows):
    chips = got.shape[0]
    depth, cols = high.shape
    return pl.pallas_call(
        ladder_kernel,
        out_shape=jax.ShapeDtypeStruct((chips * rows, cols), jnp.float32),
        in_specs=[SMEM, ANY, ANY, ANY],
        out_specs=VMEM,
        scratch_shapes=[
            pltpu.VMEM(got.shape, jnp.float32),
            pltpu.SMEM((chips, HEAD, LANES), jnp.float32),
            pltpu.SMEM((depth // LANES,), jnp.int32),
            pltpu.VMEM(high.shape, jnp.bfloat16),
            pltpu.VMEM(low.shape, jnp.bfloat16),
            pltpu.VMEM((chips * rows, depth), jnp.bfloat16),
            pltpu.VMEM((chips * rows, depth), jnp.bfloat16),
            pltpu.SemaphoreType.DMA((4,)),
        ],
        cost_estimate=pl.CostEstimate(
            flops=6 * chips * rows * depth * cols, bytes_accessed=16 << 20, transcendentals=0
        ),
        name="ladder",
    )(pos, got, high, low)


def swap_core(block):
    return lax.ppermute(block, "core", [(0, 1), (1, 0)])


def along_ring(block):
    n = lax.axis_size("grp")
    pairs = [(i, (i + 1) % n) for i in range(n)]
    pairs += [(n + i, n + (i - 1) % n) for i in range(n)]
    return lax.ppermute(block, ("core", "grp"), pairs)


def gather_panel(block):
    n = lax.axis_size("grp")
    near = [jnp.concatenate([block, swap_core(block)], axis=0)]
    swapped = []
    for _ in range(n // 2 - 1):
        near.append(along_ring(near[-1]))
        swapped.append(swap_core(near[-1]))
    far = along_ring(near[-1][: block.shape[0]])
    return near + swapped + [far, swap_core(far)]


def on_device(amplitudes, integrals, occupancy, tile_place):
    chips = NX * NZ
    per_chip = tile_place.shape[0] // chips
    rows, width = amplitudes.shape[2:]
    cols = integrals.shape[1]
    panel = gather_panel(integrals)
    sent = pack(occupancy[0], tile_place, amplitudes[0], chips, per_chip)
    got = lax.all_to_all(sent, CHIPS, 0, 0, tiled=True)
    high, low = split_panel(panel)
    pos = jnp.stack([lax.axis_index("core"), lax.axis_index("grp")]).astype(jnp.int32)
    part = ladder(pos, got, high, low, rows)
    part = part.reshape(NX, NZ * rows, cols)
    part = lax.all_to_all(part, "x", 0, 0, tiled=True).sum(axis=0)
    part = part.reshape(NZ, rows, cols)
    return lax.all_to_all(part, "z", 0, 0, tiled=True).sum(axis=0)


def solution(mesh):
    split_mesh = Mesh(mesh.devices.reshape(NX, NZ, NC, -1), EVERY)
    return jax.shard_map(
        on_device,
        mesh=split_mesh,
        in_specs=(
            P(EVERY, None, None, None),
            P(EVERY, None),
            P(EVERY, None),
            P(),
        ),
        out_specs=P(EVERY, None),
        check_vma=False,
    )
```

```python
import jax
import jax.numpy as jnp
from jax import lax
from jax.experimental import pallas as pl
from jax.experimental.pallas import tpu as pltpu
from jax.sharding import Mesh, PartitionSpec as P

NX, NZ, NC = 4, 8, 2
CAP = 4
CHIPS = ("x", "z")
EVERY = ("x", "z", "core", "grp")
LANES = 128
HEAD = 8
LATE = 4
VMEM = pl.BlockSpec(memory_space=pltpu.VMEM)
SMEM = pl.BlockSpec(memory_space=pltpu.SMEM)
ANY = pl.BlockSpec(memory_space=pl.ANY)


def panel_position(core, grp, of_core, of_grp, n):
    ahead = jnp.where(core == 0, grp - of_grp + n, of_grp - grp + n) % n
    other = jnp.where(core == of_core, 0, 1)
    near = jnp.where(ahead == 0, 0, 4 * ahead - 2) + other
    back = 4 * (n - ahead) + 1 - other
    return jnp.where(ahead <= n // 2, near, back)


def pack_kernel(pos_ref, occ_ref, place_ref, amp_ref, out_ref, count_ref, where_ref):
    rows = amp_ref.shape[1]
    per_chip = where_ref.shape[0]
    per_core = per_chip // NC
    heading = jnp.full((HEAD, LANES), per_chip, jnp.int32).astype(jnp.float32)
    lane = lax.broadcasted_iota(jnp.int32, (HEAD, LANES), 1)

    def clear(i, carry):
        count_ref[i] = 0
        out_ref[i, pl.ds(0, HEAD), :] = heading
        return carry

    lax.fori_loop(0, count_ref.shape[0], clear, 0, unroll=4)
    for core in range(NC):
        for grp in range(per_core):
            where_ref[core * per_core + grp] = panel_position(
                pos_ref[0], pos_ref[1], core, grp, per_core
            )

    def step(j, carry):
        place = place_ref[occ_ref[j]]
        chip = place // per_chip
        at = where_ref[place % per_chip]
        slot = count_ref[chip]
        count_ref[chip] = slot + 1
        out_ref[chip, pl.ds(pl.multiple_of(HEAD + slot * rows, 8), rows), :] = amp_ref[j]
        out_ref[chip, pl.ds(0, HEAD), :] = jnp.where(
            lane == slot, at.astype(jnp.float32), out_ref[chip, pl.ds(0, HEAD), :]
        )
        return carry

    lax.fori_loop(0, occ_ref.shape[0], step, 0, unroll=4)


def pack(pos, occ, place, amp, chips, per_chip):
    rows, width = amp.shape[1:]
    return pl.pallas_call(
        pack_kernel,
        out_shape=jax.ShapeDtypeStruct((chips, HEAD + NC * CAP * rows, width), jnp.float32),
        in_specs=[SMEM, SMEM, SMEM, VMEM],
        out_specs=VMEM,
        scratch_shapes=[pltpu.SMEM((chips,), jnp.int32), pltpu.SMEM((per_chip,), jnp.int32)],
        cost_estimate=pl.CostEstimate(flops=0, bytes_accessed=8 << 20, transcendentals=0),
        compiler_params=pltpu.CompilerParams(vmem_limit_bytes=8 << 20),
        name="pack",
    )(pos, occ, place, amp)


def split(value):
    high = value.astype(jnp.bfloat16)
    return high, (value - high.astype(jnp.float32)).astype(jnp.bfloat16)


def split_kernel(*refs):
    blocks, (high_ref, low_ref) = refs[:-2], refs[-2:]
    at = 0
    for ref in blocks:
        for i in range(0, ref.shape[0], 64):
            high, low = split(ref[i : i + 64, :])
            high_ref[at : at + 64, :] = high
            low_ref[at : at + 64, :] = low
            at += 64


def split_panel(blocks):
    depth = sum(block.shape[0] for block in blocks)
    out = jax.ShapeDtypeStruct((depth, blocks[0].shape[1]), jnp.bfloat16)
    return pl.pallas_call(
        split_kernel,
        out_shape=(out, out),
        in_specs=[VMEM] * len(blocks),
        out_specs=(VMEM, VMEM),
        cost_estimate=pl.CostEstimate(flops=0, bytes_accessed=8 * depth * 1024, transcendentals=0),
        compiler_params=pltpu.CompilerParams(vmem_limit_bytes=18 << 20),
        name="split_panel",
    )(*blocks)


def ladder_kernel(parts, got_hbm, *refs):
    panel_hbm, (out_ref, got, head, v_high, v_low, left, sems) = refs[: 2 * parts], refs[2 * parts :]
    chips = got.shape[0]
    rows = out_ref.shape[0] // chips
    height = out_ref.shape[0]
    depth = v_high.shape[0]
    first = [
        pltpu.make_async_copy(got_hbm.at[:, pl.ds(0, HEAD), :], head, sems.at[0]),
        pltpu.make_async_copy(got_hbm, got, sems.at[1]),
    ]
    panel = []
    at = 0
    for i in range(parts):
        size = panel_hbm[2 * i].shape[0]
        for j, ref in enumerate((v_high, v_low)):
            panel.append(
                pltpu.make_async_copy(
                    panel_hbm[2 * i + j], ref.at[pl.ds(at, size), :], sems.at[2 + 2 * i + j]
                )
            )
        at += size
    for copy in first + panel:
        copy.start()

    def clear(i, carry):
        left[pl.ds(pl.multiple_of(i * 32, 32), 32), :] = jnp.zeros((32, left.shape[1]), left.dtype)
        return carry

    lax.fori_loop(0, left.shape[0] // 32, clear, 0)
    for copy in first:
        copy.wait()

    def step(n, carry):
        row = pl.multiple_of(n * rows, rows)
        for s in range(NC * CAP):
            col = pl.multiple_of(head[n, 0, s].astype(jnp.int32) * LANES, LANES)
            high, low = split(got[n, HEAD + s * rows : HEAD + (s + 1) * rows, :])
            left[pl.ds(row, rows), pl.ds(col, LANES)] = high
            left[pl.ds(height + row, rows), pl.ds(col, LANES)] = low
        return carry

    lax.fori_loop(0, chips, step, 0, unroll=2)
    for copy in panel:
        copy.wait()
    dot = lambda a, b: jnp.dot(a, b, preferred_element_type=jnp.float32)
    wide = 256

    def columns(i, carry):
        cols = pl.ds(pl.multiple_of(i * wide, wide), wide)
        both = dot(left[:, :depth], v_high[:, cols])
        out_ref[:, cols] = both[:height] + (both[height:] + dot(left[:height, :depth], v_low[:, cols]))
        return carry

    lax.fori_loop(0, out_ref.shape[1] // wide, columns, 0)


def ladder(got, panels, rows):
    chips = got.shape[0]
    depth = sum(high.shape[0] for high, _ in panels)
    cols = panels[0][0].shape[1]
    parts = len(panels)
    return pl.pallas_call(
        lambda *refs: ladder_kernel(parts, *refs),
        out_shape=jax.ShapeDtypeStruct((chips * rows, cols), jnp.float32),
        in_specs=[ANY] * (1 + 2 * parts),
        out_specs=VMEM,
        scratch_shapes=[
            pltpu.VMEM(got.shape, jnp.float32),
            pltpu.SMEM((chips, HEAD, LANES), jnp.float32),
            pltpu.VMEM((depth, cols), jnp.bfloat16),
            pltpu.VMEM((depth, cols), jnp.bfloat16),
            pltpu.VMEM((2 * chips * rows, depth + LANES), jnp.bfloat16),
            pltpu.SemaphoreType.DMA((2 + 2 * parts,)),
        ],
        cost_estimate=pl.CostEstimate(
            flops=6 * chips * rows * depth * cols, bytes_accessed=16 << 20, transcendentals=0
        ),
        compiler_params=pltpu.CompilerParams(vmem_limit_bytes=50 << 20),
        name="ladder",
    )(got, *[half for panel in panels for half in panel])


def swap_core(block):
    return lax.ppermute(block, "core", [(0, 1), (1, 0)])


def along_ring(block):
    n = lax.axis_size("grp")
    pairs = [(i, (i + 1) % n) for i in range(n)]
    pairs += [(n + i, n + (i - 1) % n) for i in range(n)]
    return lax.ppermute(block, ("core", "grp"), pairs)


def gather_panel(block):
    n = lax.axis_size("grp")
    own, mate = block, swap_core(block)
    blocks = [own, mate]
    for _ in range(n // 2 - 1):
        own, mate = along_ring(own), along_ring(mate)
        blocks += [own, mate, swap_core(own), swap_core(mate)]
    own = along_ring(own)
    return blocks + [own, swap_core(own)]


def on_device(amplitudes, integrals, occupancy, tile_place):
    chips = NX * NZ
    per_chip = tile_place.shape[0] // chips
    rows, width = amplitudes.shape[2:]
    cols = integrals.shape[1]
    panel = gather_panel(integrals)
    pos = jnp.stack([lax.axis_index("core"), lax.axis_index("grp")]).astype(jnp.int32)
    sent = pack(pos, occupancy[0], tile_place, amplitudes[0], chips, per_chip)
    got = lax.all_to_all(sent, CHIPS, 0, 0, tiled=True)
    panels = [split_panel(panel[:-LATE]), split_panel(panel[-LATE:])]
    part = ladder(got, panels, rows)
    part = part.reshape(NX, NZ * rows, cols)
    part = lax.all_to_all(part, "x", 0, 0, tiled=True).sum(axis=0)
    part = part.reshape(NZ, rows, cols)
    return lax.all_to_all(part, "z", 0, 0, tiled=True).sum(axis=0)


def solution(mesh):
    split_mesh = Mesh(mesh.devices.reshape(NX, NZ, NC, -1), EVERY)
    return jax.shard_map(
        on_device,
        mesh=split_mesh,
        in_specs=(
            P(EVERY, None, None, None),
            P(EVERY, None),
            P(EVERY, None),
            P(),
        ),
        out_specs=P(EVERY, None),
        check_vma=False,
    )
```

```python
import jax
import jax.numpy as jnp
from jax import lax
from jax.experimental import pallas as pl
from jax.experimental.pallas import tpu as pltpu
from jax.sharding import Mesh, PartitionSpec as P

NX, NZ, NC = 4, 8, 2
CAP = 4
CHIPS = ("x", "z")
EVERY = ("x", "z", "core", "grp")
LANES = 128
HEAD = 8
BAND = 4
VMEM = pl.BlockSpec(memory_space=pltpu.VMEM)
SMEM = pl.BlockSpec(memory_space=pltpu.SMEM)
ANY = pl.BlockSpec(memory_space=pl.ANY)


def panel_position(core, grp, of_core, of_grp, n):
    ahead = jnp.where(core == 0, grp - of_grp + n, of_grp - grp + n) % n
    other = jnp.where(core == of_core, 0, 1)
    near = jnp.where(ahead == 0, 0, 4 * ahead - 2) + other
    back = 4 * (n - ahead) + 1 - other
    return jnp.where(ahead <= n // 2, near, back)


def pack_kernel(pos_ref, occ_ref, place_ref, amp_ref, out_ref, count_ref, where_ref):
    rows = amp_ref.shape[1]
    per_chip = where_ref.shape[0]
    per_core = per_chip // NC
    heading = jnp.full((HEAD, LANES), per_chip, jnp.int32).astype(jnp.float32)
    lane = lax.broadcasted_iota(jnp.int32, (HEAD, LANES), 1)

    def clear(i, carry):
        count_ref[i] = 0
        out_ref[i, pl.ds(0, HEAD), :] = heading
        return carry

    lax.fori_loop(0, count_ref.shape[0], clear, 0, unroll=4)
    for core in range(NC):
        for grp in range(per_core):
            where_ref[core * per_core + grp] = panel_position(
                pos_ref[0], pos_ref[1], core, grp, per_core
            )

    def step(j, carry):
        place = place_ref[occ_ref[j]]
        chip = place // per_chip
        at = where_ref[place % per_chip]
        slot = count_ref[chip]
        count_ref[chip] = slot + 1
        out_ref[chip, pl.ds(pl.multiple_of(HEAD + slot * rows, 8), rows), :] = amp_ref[j]
        out_ref[chip, pl.ds(0, HEAD), :] = jnp.where(
            lane == slot, at.astype(jnp.float32), out_ref[chip, pl.ds(0, HEAD), :]
        )
        return carry

    lax.fori_loop(0, occ_ref.shape[0], step, 0, unroll=4)


def pack(pos, occ, place, amp, chips, per_chip):
    rows, width = amp.shape[1:]
    return pl.pallas_call(
        pack_kernel,
        out_shape=jax.ShapeDtypeStruct((chips, HEAD + NC * CAP * rows, width), jnp.float32),
        in_specs=[SMEM, SMEM, SMEM, VMEM],
        out_specs=VMEM,
        scratch_shapes=[pltpu.SMEM((chips,), jnp.int32), pltpu.SMEM((per_chip,), jnp.int32)],
        cost_estimate=pl.CostEstimate(flops=0, bytes_accessed=8 << 20, transcendentals=0),
        name="pack",
    )(pos, occ, place, amp)


def split(value):
    high = value.astype(jnp.bfloat16)
    return high, (value - high.astype(jnp.float32)).astype(jnp.bfloat16)


def split_kernel(*refs):
    blocks, (high_ref, low_ref) = refs[:-2], refs[-2:]
    at = 0
    for ref in blocks:
        for i in range(0, ref.shape[0], 64):
            high, low = split(ref[i : i + 64, :])
            high_ref[at : at + 64, :] = high
            low_ref[at : at + 64, :] = low
            at += 64


def split_panel(blocks):
    depth = sum(block.shape[0] for block in blocks)
    out = jax.ShapeDtypeStruct((depth, blocks[0].shape[1]), jnp.bfloat16)
    return pl.pallas_call(
        split_kernel,
        out_shape=(out, out),
        in_specs=[VMEM] * len(blocks),
        out_specs=(VMEM, VMEM),
        cost_estimate=pl.CostEstimate(flops=0, bytes_accessed=8 * depth * 1024, transcendentals=0),
        compiler_params=pltpu.CompilerParams(vmem_limit_bytes=18 << 20),
        name="split_panel",
    )(*blocks)


def ladder_kernel(parts, got_hbm, *refs):
    panel_hbm, (out_hbm, got, head, v_high, v_low, left, total, sems, out_sems) = (
        refs[: 2 * parts],
        refs[2 * parts :],
    )
    chips = got.shape[0]
    height = total.shape[0]
    rows = height // chips
    first = [
        pltpu.make_async_copy(got_hbm.at[:, pl.ds(0, HEAD), :], head, sems.at[0]),
        pltpu.make_async_copy(got_hbm, got, sems.at[1]),
    ]
    panel = []
    starts = [0]
    for i in range(parts):
        size = panel_hbm[2 * i].shape[0]
        for j, ref in enumerate((v_high, v_low)):
            panel.append(
                pltpu.make_async_copy(
                    panel_hbm[2 * i + j],
                    ref.at[pl.ds(starts[-1], size), :],
                    sems.at[2 + 2 * i + j],
                )
            )
        starts.append(starts[-1] + size)
    for copy in first + panel:
        copy.start()

    def clear(i, carry):
        left[pl.ds(pl.multiple_of(i * 32, 32), 32), :] = jnp.zeros((32, left.shape[1]), left.dtype)
        return carry

    lax.fori_loop(0, left.shape[0] // 32, clear, 0)
    for copy in first:
        copy.wait()

    def step(n, carry):
        row = pl.multiple_of(n * rows, rows)
        for s in range(NC * CAP):
            col = pl.multiple_of(head[n, 0, s].astype(jnp.int32) * LANES, LANES)
            high, low = split(got[n, HEAD + s * rows : HEAD + (s + 1) * rows, :])
            left[pl.ds(row, rows), pl.ds(col, LANES)] = high
            left[pl.ds(height + row, rows), pl.ds(col, LANES)] = low
        return carry

    lax.fori_loop(0, chips, step, 0, unroll=2)
    dot = lambda a, b: jnp.dot(a, b, preferred_element_type=jnp.float32)
    wide = 256
    steps = total.shape[1] // wide

    def product(lo, hi, cols):
        both = dot(left[:, lo:hi], v_high[lo:hi, cols])
        return both[:height] + (both[height:] + dot(left[:height, lo:hi], v_low[lo:hi, cols]))

    middle = parts // 2
    for copy in panel[: 2 * middle]:
        copy.wait()

    def near(i, carry):
        cols = pl.ds(pl.multiple_of(i * wide, wide), wide)
        total[:, cols] = product(0, starts[middle], cols)
        return carry

    lax.fori_loop(0, steps, near, 0)
    for copy in panel[2 * middle :]:
        copy.wait()
    done = []
    for i in range(steps):
        cols = pl.ds(i * wide, wide)
        total[:, cols] += product(starts[middle], starts[parts], cols)
        done.append(pltpu.make_async_copy(total.at[:, cols], out_hbm.at[:, cols], out_sems.at[i]))
        done[-1].start()
    for copy in done:
        copy.wait()


def ladder(got, panels, rows):
    chips = got.shape[0]
    depth = sum(high.shape[0] for high, _ in panels)
    cols = panels[0][0].shape[1]
    parts = len(panels)
    return pl.pallas_call(
        lambda *refs: ladder_kernel(parts, *refs),
        out_shape=jax.ShapeDtypeStruct((chips * rows, cols), jnp.float32),
        in_specs=[ANY] * (1 + 2 * parts),
        out_specs=ANY,
        scratch_shapes=[
            pltpu.VMEM(got.shape, jnp.float32),
            pltpu.SMEM((chips, HEAD, LANES), jnp.float32),
            pltpu.VMEM((depth, cols), jnp.bfloat16),
            pltpu.VMEM((depth, cols), jnp.bfloat16),
            pltpu.VMEM((2 * chips * rows, depth + LANES), jnp.bfloat16),
            pltpu.VMEM((chips * rows, cols), jnp.float32),
            pltpu.SemaphoreType.DMA((2 + 2 * parts,)),
            pltpu.SemaphoreType.DMA((cols // 256,)),
        ],
        cost_estimate=pl.CostEstimate(
            flops=6 * chips * rows * depth * cols, bytes_accessed=16 << 20, transcendentals=0
        ),
        compiler_params=pltpu.CompilerParams(vmem_limit_bytes=50 << 20),
        name="ladder",
    )(got, *[half for panel in panels for half in panel])


def swap_core(block):
    return lax.ppermute(block, "core", [(0, 1), (1, 0)])


def along_ring(block):
    n = lax.axis_size("grp")
    pairs = [(i, (i + 1) % n) for i in range(n)]
    pairs += [(n + i, n + (i - 1) % n) for i in range(n)]
    return lax.ppermute(block, ("core", "grp"), pairs)


def gather_panel(own, mate):
    n = lax.axis_size("grp")
    blocks = [own, mate]
    for _ in range(n // 2 - 1):
        own, mate = along_ring(own), along_ring(mate)
        blocks += [own, mate, swap_core(own), swap_core(mate)]
    own = along_ring(own)
    return blocks + [own, swap_core(own)]


def on_device(amplitudes, integrals, occupancy, tile_place):
    chips = NX * NZ
    per_chip = tile_place.shape[0] // chips
    rows, width = amplitudes.shape[2:]
    cols = integrals.shape[1]
    mate = swap_core(integrals)
    pos = jnp.stack([lax.axis_index("core"), lax.axis_index("grp")]).astype(jnp.int32)
    sent = pack(pos, occupancy[0], tile_place, amplitudes[0], chips, per_chip)
    sent, mate = lax.optimization_barrier((sent, mate))
    panel = gather_panel(integrals, mate)
    got = lax.all_to_all(sent, CHIPS, 0, 0, tiled=True)
    panels = [split_panel(panel[i : i + BAND]) for i in range(0, len(panel), BAND)]
    part = ladder(got, panels, rows)
    part = part.reshape(NX, NZ * rows, cols)
    part = lax.all_to_all(part, "x", 0, 0, tiled=True).sum(axis=0)
    part = part.reshape(NZ, rows, cols)
    return lax.all_to_all(part, "z", 0, 0, tiled=True).sum(axis=0)


def solution(mesh):
    split_mesh = Mesh(mesh.devices.reshape(NX, NZ, NC, -1), EVERY)
    return jax.shard_map(
        on_device,
        mesh=split_mesh,
        in_specs=(
            P(EVERY, None, None, None),
            P(EVERY, None),
            P(EVERY, None),
            P(),
        ),
        out_specs=P(EVERY, None),
        check_vma=False,
    )
```

```python
import jax
import jax.numpy as jnp
from jax import lax
from jax.experimental import pallas as pl
from jax.experimental.pallas import tpu as pltpu
from jax.sharding import Mesh, PartitionSpec as P

NX, NZ, NC = 4, 8, 2
CAP = 4
CHIPS = ("x", "z")
EVERY = ("x", "z", "core", "grp")
LANES = 128
HEAD = 8
VMEM = pl.BlockSpec(memory_space=pltpu.VMEM)
SMEM = pl.BlockSpec(memory_space=pltpu.SMEM)
ANY = pl.BlockSpec(memory_space=pl.ANY)


def panel_position(core, grp, of_core, of_grp, n):
    ahead = jnp.where(core == 0, grp - of_grp + n, of_grp - grp + n) % n
    other = jnp.where(core == of_core, 0, 1)
    near = jnp.where(ahead == 0, 0, 4 * ahead - 2) + other
    back = 4 * (n - ahead) + 1 - other
    return jnp.where(ahead <= n // 2, near, back)


def pack_kernel(pos_ref, occ_ref, place_ref, amp_ref, out_ref, count_ref, where_ref):
    rows = amp_ref.shape[1]
    per_chip = where_ref.shape[0]
    per_core = per_chip // NC
    heading = jnp.full((HEAD, LANES), per_chip, jnp.int32).astype(jnp.float32)
    lane = lax.broadcasted_iota(jnp.int32, (HEAD, LANES), 1)

    def clear(i, carry):
        count_ref[i] = 0
        out_ref[i, pl.ds(0, HEAD), :] = heading
        return carry

    lax.fori_loop(0, count_ref.shape[0], clear, 0, unroll=4)
    for core in range(NC):
        for grp in range(per_core):
            where_ref[core * per_core + grp] = panel_position(
                pos_ref[0], pos_ref[1], core, grp, per_core
            )

    def step(j, carry):
        place = place_ref[occ_ref[j]]
        chip = place // per_chip
        at = where_ref[place % per_chip]
        slot = count_ref[chip]
        count_ref[chip] = slot + 1
        out_ref[chip, pl.ds(pl.multiple_of(HEAD + slot * rows, 8), rows), :] = amp_ref[j]
        out_ref[chip, pl.ds(0, HEAD), :] = jnp.where(
            lane == slot, at.astype(jnp.float32), out_ref[chip, pl.ds(0, HEAD), :]
        )
        return carry

    lax.fori_loop(0, occ_ref.shape[0], step, 0, unroll=4)


def pack(pos, occ, place, amp, chips, per_chip):
    rows, width = amp.shape[1:]
    return pl.pallas_call(
        pack_kernel,
        out_shape=jax.ShapeDtypeStruct((chips, HEAD + NC * CAP * rows, width), jnp.float32),
        in_specs=[SMEM, SMEM, SMEM, VMEM],
        out_specs=VMEM,
        scratch_shapes=[pltpu.SMEM((chips,), jnp.int32), pltpu.SMEM((per_chip,), jnp.int32)],
        cost_estimate=pl.CostEstimate(flops=0, bytes_accessed=8 << 20, transcendentals=0),
        name="pack",
    )(pos, occ, place, amp)


def split(value):
    high = value.astype(jnp.bfloat16)
    return high, (value - high.astype(jnp.float32)).astype(jnp.bfloat16)


def ladder_kernel(pieces, got_hbm, *refs):
    blocks = len({piece[0] for piece in pieces})
    panel_hbm, (out_hbm, got, head, panel, v_high, v_low, left, total, sems, out_sems) = (
        refs[:blocks],
        refs[blocks:],
    )
    chips = got.shape[0]
    height = total.shape[0]
    rows = height // chips
    depth = panel.shape[0]
    first = [
        pltpu.make_async_copy(got_hbm.at[:, pl.ds(0, HEAD), :], head, sems.at[0]),
        pltpu.make_async_copy(got_hbm, got, sems.at[1]),
    ]
    halves = ([], [])
    at = 0
    for i, (block, start, size) in enumerate(pieces):
        copy = pltpu.make_async_copy(
            panel_hbm[block].at[pl.ds(start, size), :],
            panel.at[pl.ds(at, size), :],
            sems.at[2 + i],
        )
        halves[at * 2 // depth].append(copy)
        at += size
    for copy in first + halves[0] + halves[1]:
        copy.start()

    def clear(i, carry):
        left[pl.ds(pl.multiple_of(i * 32, 32), 32), :] = jnp.zeros((32, left.shape[1]), left.dtype)
        return carry

    lax.fori_loop(0, left.shape[0] // 32, clear, 0)
    for copy in first:
        copy.wait()

    def step(n, carry):
        row = pl.multiple_of(n * rows, rows)
        for s in range(NC * CAP):
            col = pl.multiple_of(head[n, 0, s].astype(jnp.int32) * LANES, LANES)
            high, low = split(got[n, HEAD + s * rows : HEAD + (s + 1) * rows, :])
            left[pl.ds(row, rows), pl.ds(col, LANES)] = high
            left[pl.ds(height + row, rows), pl.ds(col, LANES)] = low
        return carry

    lax.fori_loop(0, chips, step, 0, unroll=2)
    dot = lambda a, b: jnp.dot(a, b, preferred_element_type=jnp.float32)
    wide = 256
    steps = total.shape[1] // wide
    done = []
    for which in range(2):
        lo, hi = which * depth // 2, (which + 1) * depth // 2
        for copy in halves[which]:
            copy.wait()

        def split_rows(i, carry):
            at = pl.ds(pl.multiple_of(lo + i * 32, 32), 32)
            v_high[at, :], v_low[at, :] = split(panel[at, :])
            return carry

        lax.fori_loop(0, (hi - lo) // 32, split_rows, 0)
        for i in range(steps):
            cols = pl.ds(i * wide, wide)
            both = dot(left[:, lo:hi], v_high[lo:hi, cols])
            part = both[:height] + (both[height:] + dot(left[:height, lo:hi], v_low[lo:hi, cols]))
            if which == 0:
                total[:, cols] = part
            else:
                total[:, cols] += part
                done.append(
                    pltpu.make_async_copy(total.at[:, cols], out_hbm.at[:, cols], out_sems.at[i])
                )
                done[-1].start()
    for copy in done:
        copy.wait()


def ladder(got, blocks, pieces, rows):
    chips = got.shape[0]
    depth = sum(size for _, _, size in pieces)
    cols = blocks[0].shape[1]
    return pl.pallas_call(
        lambda *refs: ladder_kernel(pieces, *refs),
        out_shape=jax.ShapeDtypeStruct((chips * rows, cols), jnp.float32),
        in_specs=[ANY] * (1 + len(blocks)),
        out_specs=ANY,
        scratch_shapes=[
            pltpu.VMEM(got.shape, jnp.float32),
            pltpu.SMEM((chips, HEAD, LANES), jnp.float32),
            pltpu.VMEM((depth, cols), jnp.float32),
            pltpu.VMEM((depth, cols), jnp.bfloat16),
            pltpu.VMEM((depth, cols), jnp.bfloat16),
            pltpu.VMEM((2 * chips * rows, depth + LANES), jnp.bfloat16),
            pltpu.VMEM((chips * rows, cols), jnp.float32),
            pltpu.SemaphoreType.DMA((2 + len(pieces),)),
            pltpu.SemaphoreType.DMA((cols // 256,)),
        ],
        cost_estimate=pl.CostEstimate(
            flops=6 * chips * rows * depth * cols, bytes_accessed=16 << 20, transcendentals=0
        ),
        compiler_params=pltpu.CompilerParams(vmem_limit_bytes=50 << 20),
        name="ladder",
    )(got, *blocks)


def swap_core(block):
    return lax.ppermute(block, "core", [(0, 1), (1, 0)])


def along_ring(block):
    n = lax.axis_size("grp")
    pairs = [(i, (i + 1) % n) for i in range(n)]
    pairs += [(n + i, n + (i - 1) % n) for i in range(n)]
    return lax.ppermute(block, ("core", "grp"), pairs)


def gather_panel(own, mate):
    n = lax.axis_size("grp")
    size = own.shape[0]
    blocks, pieces = [], []

    def place(block, start=0, length=None):
        for known, other in enumerate(blocks):
            if other is block:
                break
        else:
            known = len(blocks)
            blocks.append(block)
        pieces.append((known, start, length or block.shape[0]))

    place(own)
    place(mate)
    for _ in range(n // 2 - 1):
        own, mate = along_ring(own), along_ring(mate)
        place(own)
        place(mate)
        place(swap_core(jnp.concatenate([own, mate], axis=0)))
    half = size // 2
    top, bottom = along_ring(own[:half]), along_ring(mate[half:])
    swapped = swap_core(jnp.concatenate([top, bottom], axis=0))
    place(top)
    place(swapped, half, half)
    place(swapped, 0, half)
    place(bottom)
    return blocks, pieces


def on_device(amplitudes, integrals, occupancy, tile_place):
    chips = NX * NZ
    per_chip = tile_place.shape[0] // chips
    rows, width = amplitudes.shape[2:]
    cols = integrals.shape[1]
    mate = swap_core(integrals)
    pos = jnp.stack([lax.axis_index("core"), lax.axis_index("grp")]).astype(jnp.int32)
    sent = pack(pos, occupancy[0], tile_place, amplitudes[0], chips, per_chip)
    sent, mate = lax.optimization_barrier((sent, mate))
    blocks, pieces = gather_panel(integrals, mate)
    got = lax.all_to_all(sent, CHIPS, 0, 0, tiled=True)
    part = ladder(got, blocks, pieces, rows)
    part = part.reshape(NX, NZ * rows, cols)
    part = lax.all_to_all(part, "x", 0, 0, tiled=True).sum(axis=0)
    part = part.reshape(NZ, rows, cols)
    return lax.all_to_all(part, "z", 0, 0, tiled=True).sum(axis=0)


def solution(mesh):
    split_mesh = Mesh(mesh.devices.reshape(NX, NZ, NC, -1), EVERY)
    return jax.shard_map(
        on_device,
        mesh=split_mesh,
        in_specs=(
            P(EVERY, None, None, None),
            P(EVERY, None),
            P(EVERY, None),
            P(),
        ),
        out_specs=P(EVERY, None),
        check_vma=False,
    )
```

```python
import jax
import jax.numpy as jnp
from jax import lax
from jax.experimental import pallas as pl
from jax.experimental.pallas import tpu as pltpu
from jax.sharding import Mesh, PartitionSpec as P

NX, NZ, NC = 4, 8, 2
CAP = 4
CHIPS = ("x", "z")
EVERY = ("x", "z", "core", "grp")
LANES = 128
HEAD = 8
EARLY = 10
VMEM_LIMIT = 20 << 20
VMEM = pl.BlockSpec(memory_space=pltpu.VMEM)
SMEM = pl.BlockSpec(memory_space=pltpu.SMEM)
ANY = pl.BlockSpec(memory_space=pl.ANY)


def panel_position(core, grp, of_core, of_grp, n):
    ahead = jnp.where(core == 0, grp - of_grp + n, of_grp - grp + n) % n
    other = jnp.where(core == of_core, 0, 1)
    near = jnp.where(ahead == 0, 0, 4 * ahead - 2) + other
    back = 4 * (n - ahead) + 1 - other
    return jnp.where(ahead <= n // 2, near, back)


def pack_kernel(occ_ref, place_ref, amp_ref, out_ref, count_ref, where_ref):
    rows = amp_ref.shape[1]
    per_chip = where_ref.shape[0]
    per_core = per_chip // NC
    here = lax.axis_index("core"), lax.axis_index("grp")
    heading = jnp.full((HEAD, LANES), per_chip, jnp.int32).astype(jnp.float32)
    lane = lax.broadcasted_iota(jnp.int32, (HEAD, LANES), 1)

    def clear(i, carry):
        count_ref[i] = 0
        out_ref[i, pl.ds(0, HEAD), :] = heading
        return carry

    lax.fori_loop(0, count_ref.shape[0], clear, 0, unroll=4)
    for core in range(NC):
        for grp in range(per_core):
            where_ref[core * per_core + grp] = panel_position(*here, core, grp, per_core)

    def step(j, carry):
        place = place_ref[occ_ref[j]]
        chip = place // per_chip
        at = where_ref[place % per_chip]
        slot = count_ref[chip]
        count_ref[chip] = slot + 1
        out_ref[chip, pl.ds(pl.multiple_of(HEAD + slot * rows, 8), rows), :] = amp_ref[j]
        out_ref[chip, pl.ds(0, HEAD), :] = jnp.where(
            lane == slot, at.astype(jnp.float32), out_ref[chip, pl.ds(0, HEAD), :]
        )
        return carry

    lax.fori_loop(0, occ_ref.shape[0], step, 0, unroll=4)


def pack(occ, place, amp, chips, per_chip):
    rows, width = amp.shape[1:]
    return pl.pallas_call(
        pack_kernel,
        out_shape=jax.ShapeDtypeStruct((chips, HEAD + NC * CAP * rows, width), jnp.float32),
        in_specs=[SMEM, SMEM, VMEM],
        out_specs=VMEM,
        scratch_shapes=[pltpu.SMEM((chips,), jnp.int32), pltpu.SMEM((per_chip,), jnp.int32)],
        cost_estimate=pl.CostEstimate(flops=0, bytes_accessed=8 << 20, transcendentals=0),
        name="pack",
    )(occ, place, amp)


def split(value):
    high = value.astype(jnp.bfloat16)
    return high, (value - high.astype(jnp.float32)).astype(jnp.bfloat16)


def spread_kernel(got_ref, left_ref, head, sem):
    chips = got_ref.shape[0]
    height = left_ref.shape[0] // 2
    rows = height // chips
    copy = pltpu.make_async_copy(got_ref.at[:, pl.ds(0, HEAD), :], head, sem)
    copy.start()

    def clear(i, carry):
        at = pl.ds(pl.multiple_of(i * 32, 32), 32)
        left_ref[at, :] = jnp.zeros((32, left_ref.shape[1]), left_ref.dtype)
        return carry

    lax.fori_loop(0, left_ref.shape[0] // 32, clear, 0)
    copy.wait()

    def step(n, carry):
        row = pl.multiple_of(n * rows, rows)
        for s in range(NC * CAP):
            col = pl.multiple_of(head[n, 0, s].astype(jnp.int32) * LANES, LANES)
            high, low = split(got_ref[n, HEAD + s * rows : HEAD + (s + 1) * rows, :])
            left_ref[pl.ds(row, rows), pl.ds(col, LANES)] = high
            left_ref[pl.ds(height + row, rows), pl.ds(col, LANES)] = low
        return carry

    lax.fori_loop(0, chips, step, 0, unroll=2)


def spread(got, rows, depth):
    chips = got.shape[0]
    return pl.pallas_call(
        spread_kernel,
        out_shape=jax.ShapeDtypeStruct((2 * chips * rows, depth + LANES), jnp.bfloat16),
        in_specs=[VMEM],
        out_specs=VMEM,
        scratch_shapes=[
            pltpu.SMEM((chips, HEAD, LANES), jnp.float32),
            pltpu.SemaphoreType.DMA,
        ],
        cost_estimate=pl.CostEstimate(flops=0, bytes_accessed=8 << 20, transcendentals=0),
        compiler_params=pltpu.CompilerParams(vmem_limit_bytes=VMEM_LIMIT),
        name="spread",
    )(got)


def product_kernel(pieces, start, has_total, *refs):
    left_ref, refs = refs[0], refs[1:]
    if has_total:
        total_ref, refs = refs[0], refs[1:]
    panel, (out_ref, v_high, v_low) = refs[:-3], refs[-3:]
    height = out_ref.shape[0]
    depth = v_high.shape[0]
    at = 0
    for block, first, size in pieces:
        for i in range(0, size, 64):
            value = panel[block][first + i : first + i + 64, :]
            v_high[at : at + 64, :], v_low[at : at + 64, :] = split(value)
            at += 64
    dot = lambda a, b: jnp.dot(a, b, preferred_element_type=jnp.float32)
    wide = 256
    for i in range(0, out_ref.shape[1], wide):
        cols = pl.ds(i, wide)
        both = dot(left_ref[:, start : start + depth], v_high[:, cols])
        part = both[height:] + dot(left_ref[:height, start : start + depth], v_low[:, cols])
        part = both[:height] + part
        out_ref[:, cols] = part + total_ref[:, cols] if has_total else part


def product(left, start, blocks, pieces, total=None):
    height = left.shape[0] // 2
    depth = sum(size for _, _, size in pieces)
    cols = blocks[0].shape[1]
    used = sorted({piece[0] for piece in pieces})
    pieces = [(used.index(block), first, size) for block, first, size in pieces]
    extra = [] if total is None else [total]
    operands = [left] + extra + [blocks[i] for i in used]
    return pl.pallas_call(
        lambda *refs: product_kernel(pieces, start, bool(extra), *refs),
        out_shape=jax.ShapeDtypeStruct((height, cols), jnp.float32),
        in_specs=[VMEM] * len(operands),
        out_specs=VMEM,
        scratch_shapes=[
            pltpu.VMEM((depth, cols), jnp.bfloat16),
            pltpu.VMEM((depth, cols), jnp.bfloat16),
        ],
        cost_estimate=pl.CostEstimate(
            flops=6 * height * depth * cols, bytes_accessed=4 << 20, transcendentals=0
        ),
        compiler_params=pltpu.CompilerParams(vmem_limit_bytes=VMEM_LIMIT),
        name="product",
    )(*operands)


def swap_core(block):
    return lax.ppermute(block, "core", [(0, 1), (1, 0)])


def along_ring(block, cross=False):
    n = lax.axis_size("grp")
    up, down = (n, 0) if cross else (0, n)
    pairs = [(up + i, (i + 1) % n) for i in range(n)]
    pairs += [(down + i, n + (i - 1) % n) for i in range(n)]
    return lax.ppermute(block, ("core", "grp"), pairs)


def gather_panel(block):
    n = lax.axis_size("grp")
    size = block.shape[0]
    blocks, pieces = [], []

    def place(block, start=0, length=None):
        for known, other in enumerate(blocks):
            if other is block:
                break
        else:
            known = len(blocks)
            blocks.append(block)
        pieces.append((known, start, length or block.shape[0]))

    place(block)
    place(swap_core(block))
    for step in range(n // 2 - 1):
        own = along_ring(own if step else block)
        mate = along_ring(mate) if step else along_ring(block, cross=True)
        place(own)
        place(mate)
        place(swap_core(jnp.concatenate([own, mate], axis=0)))
    half = size // 2
    top, bottom = along_ring(own[:half]), along_ring(mate[half:])
    swapped = swap_core(jnp.concatenate([top, bottom], axis=0))
    place(top)
    place(swapped, half, half)
    place(swapped, 0, half)
    place(bottom)
    return blocks, pieces


def on_device(amplitudes, integrals, occupancy, tile_place):
    chips = NX * NZ
    per_chip = tile_place.shape[0] // chips
    rows, width = amplitudes.shape[2:]
    cols = integrals.shape[1]
    sent = pack(occupancy[0], tile_place, amplitudes[0], chips, per_chip)
    got = lax.all_to_all(sent, CHIPS, 0, 0, tiled=True)
    blocks, pieces = gather_panel(integrals)
    left = spread(got, rows, per_chip * width)
    early, depth = 0, 0
    while depth < EARLY * width:
        depth += pieces[early][2]
        early += 1
    part = product(left, 0, blocks, pieces[:early])
    part = product(left, depth, blocks, pieces[early:], part)
    part = part.reshape(NX, NZ * rows, cols)
    part = lax.all_to_all(part, "x", 0, 0, tiled=True).sum(axis=0)
    part = part.reshape(NZ, rows, cols)
    return lax.all_to_all(part, "z", 0, 0, tiled=True).sum(axis=0)


def solution(mesh):
    split_mesh = Mesh(mesh.devices.reshape(NX, NZ, NC, -1), EVERY)
    return jax.shard_map(
        on_device,
        mesh=split_mesh,
        in_specs=(
            P(EVERY, None, None, None),
            P(EVERY, None),
            P(EVERY, None),
            P(),
        ),
        out_specs=P(EVERY, None),
        check_vma=False,
    )
```

```python
import jax
import jax.numpy as jnp
from jax import lax
from jax.experimental import pallas as pl
from jax.experimental.pallas import tpu as pltpu
from jax.sharding import Mesh, PartitionSpec as P

NX, NZ, NC = 4, 8, 2
CAP = 4
CHIPS = ("x", "z")
EVERY = ("x", "z", "core", "grp")
LANES = 128
HEAD = 8
EARLY = 12
VMEM_LIMIT = 20 << 20
VMEM = pl.BlockSpec(memory_space=pltpu.VMEM)
SMEM = pl.BlockSpec(memory_space=pltpu.SMEM)
ANY = pl.BlockSpec(memory_space=pl.ANY)


def panel_position(core, grp, of_core, of_grp, n):
    ahead = jnp.where(core == 0, grp - of_grp + n, of_grp - grp + n) % n
    other = jnp.where(core == of_core, 0, 1)
    near = jnp.where(ahead == 0, 0, 4 * ahead - 2) + other
    back = 4 * (n - ahead) + 1 - other
    return jnp.where(ahead <= n // 2, near, back)


def pack_kernel(occ_ref, place_ref, amp_ref, out_ref, count_ref, where_ref):
    rows = amp_ref.shape[1]
    per_chip = where_ref.shape[0]
    per_core = per_chip // NC
    here = lax.axis_index("core"), lax.axis_index("grp")
    heading = jnp.full((HEAD, LANES), per_chip, jnp.int32).astype(jnp.float32)
    lane = lax.broadcasted_iota(jnp.int32, (HEAD, LANES), 1)

    def clear(i, carry):
        count_ref[i] = 0
        out_ref[i, pl.ds(0, HEAD), :] = heading
        return carry

    lax.fori_loop(0, count_ref.shape[0], clear, 0, unroll=4)
    for core in range(NC):
        for grp in range(per_core):
            where_ref[core * per_core + grp] = panel_position(*here, core, grp, per_core)

    def step(j, carry):
        place = place_ref[occ_ref[j]]
        chip = place // per_chip
        at = where_ref[place % per_chip]
        slot = count_ref[chip]
        count_ref[chip] = slot + 1
        out_ref[chip, pl.ds(pl.multiple_of(HEAD + slot * rows, 8), rows), :] = amp_ref[j]
        out_ref[chip, pl.ds(0, HEAD), :] = jnp.where(
            lane == slot, at.astype(jnp.float32), out_ref[chip, pl.ds(0, HEAD), :]
        )
        return carry

    lax.fori_loop(0, occ_ref.shape[0], step, 0, unroll=4)


def pack(occ, place, amp, chips, per_chip):
    rows, width = amp.shape[1:]
    return pl.pallas_call(
        pack_kernel,
        out_shape=jax.ShapeDtypeStruct((chips, HEAD + NC * CAP * rows, width), jnp.float32),
        in_specs=[SMEM, SMEM, VMEM],
        out_specs=VMEM,
        scratch_shapes=[pltpu.SMEM((chips,), jnp.int32), pltpu.SMEM((per_chip,), jnp.int32)],
        cost_estimate=pl.CostEstimate(flops=0, bytes_accessed=8 << 20, transcendentals=0),
        name="pack",
    )(occ, place, amp)


def split(value):
    high = value.astype(jnp.bfloat16)
    return high, (value - high.astype(jnp.float32)).astype(jnp.bfloat16)


def spread_kernel(got_ref, left_ref, head, sem):
    chips = got_ref.shape[0]
    height = left_ref.shape[0] // 2
    rows = height // chips
    copy = pltpu.make_async_copy(got_ref.at[:, pl.ds(0, HEAD), :], head, sem)
    copy.start()

    def clear(i, carry):
        at = pl.ds(pl.multiple_of(i * 32, 32), 32)
        left_ref[at, :] = jnp.zeros((32, left_ref.shape[1]), left_ref.dtype)
        return carry

    lax.fori_loop(0, left_ref.shape[0] // 32, clear, 0)
    copy.wait()

    def step(n, carry):
        row = pl.multiple_of(n * rows, rows)
        for s in range(NC * CAP):
            col = pl.multiple_of(head[n, 0, s].astype(jnp.int32) * LANES, LANES)
            high, low = split(got_ref[n, HEAD + s * rows : HEAD + (s + 1) * rows, :])
            left_ref[pl.ds(row, rows), pl.ds(col, LANES)] = high
            left_ref[pl.ds(height + row, rows), pl.ds(col, LANES)] = low
        return carry

    lax.fori_loop(0, chips, step, 0, unroll=2)


def spread(got, rows, depth):
    chips = got.shape[0]
    return pl.pallas_call(
        spread_kernel,
        out_shape=jax.ShapeDtypeStruct((2 * chips * rows, depth + LANES), jnp.bfloat16),
        in_specs=[VMEM],
        out_specs=VMEM,
        scratch_shapes=[
            pltpu.SMEM((chips, HEAD, LANES), jnp.float32),
            pltpu.SemaphoreType.DMA,
        ],
        cost_estimate=pl.CostEstimate(flops=0, bytes_accessed=8 << 20, transcendentals=0),
        compiler_params=pltpu.CompilerParams(vmem_limit_bytes=VMEM_LIMIT),
        name="spread",
    )(got)


def product_kernel(pieces, start, has_total, *refs):
    left_ref, refs = refs[0], refs[1:]
    if has_total:
        total_ref, refs = refs[0], refs[1:]
    panel, (out_ref, v_high, v_low) = refs[:-3], refs[-3:]
    height = out_ref.shape[0]
    depth = v_high.shape[0]
    at = 0
    for block, first, size in pieces:
        for i in range(0, size, 64):
            value = panel[block][first + i : first + i + 64, :]
            v_high[at : at + 64, :], v_low[at : at + 64, :] = split(value)
            at += 64
    dot = lambda a, b: jnp.dot(a, b, preferred_element_type=jnp.float32)
    wide = 256
    for i in range(0, out_ref.shape[1], wide):
        cols = pl.ds(i, wide)
        both = dot(left_ref[:, start : start + depth], v_high[:, cols])
        part = both[height:] + dot(left_ref[:height, start : start + depth], v_low[:, cols])
        part = both[:height] + part
        out_ref[:, cols] = part + total_ref[:, cols] if has_total else part


def product(left, start, blocks, pieces, total=None):
    height = left.shape[0] // 2
    depth = sum(size for _, _, size in pieces)
    cols = blocks[0].shape[1]
    used = sorted({piece[0] for piece in pieces})
    pieces = [(used.index(block), first, size) for block, first, size in pieces]
    extra = [] if total is None else [total]
    operands = [left] + extra + [blocks[i] for i in used]
    return pl.pallas_call(
        lambda *refs: product_kernel(pieces, start, bool(extra), *refs),
        out_shape=jax.ShapeDtypeStruct((height, cols), jnp.float32),
        in_specs=[VMEM] * len(operands),
        out_specs=VMEM,
        scratch_shapes=[
            pltpu.VMEM((depth, cols), jnp.bfloat16),
            pltpu.VMEM((depth, cols), jnp.bfloat16),
        ],
        cost_estimate=pl.CostEstimate(
            flops=6 * height * depth * cols, bytes_accessed=4 << 20, transcendentals=0
        ),
        compiler_params=pltpu.CompilerParams(vmem_limit_bytes=VMEM_LIMIT),
        name="product",
    )(*operands)


def swap_core(block):
    return lax.ppermute(block, "core", [(0, 1), (1, 0)])


def along_ring(block, cross=False):
    n = lax.axis_size("grp")
    up, down = (n, 0) if cross else (0, n)
    pairs = [(up + i, (i + 1) % n) for i in range(n)]
    pairs += [(down + i, n + (i - 1) % n) for i in range(n)]
    return lax.ppermute(block, ("core", "grp"), pairs)


def gather_panel(block, after):
    n = lax.axis_size("grp")
    size = block.shape[0]
    half = size // 2
    own, mate = along_ring(block), along_ring(block, cross=True)
    swapped = swap_core(block)
    blocks = [block, swapped]
    for step in range(1, n // 2):
        blocks += [own, mate]
        held, _ = lax.optimization_barrier((mate, swapped))
        if step < n // 2 - 1:
            swapped = swap_core(jnp.concatenate([own, mate], axis=0))
            blocks.append(swapped)
            own, mate = along_ring(own), along_ring(held)
    top, bottom = along_ring(own[:half]), along_ring(held[half:])
    held, _ = lax.optimization_barrier((top, after))
    blocks.append(swap_core(jnp.concatenate([own, mate, held, bottom], axis=0)))
    pieces = [(i, 0, b.shape[0]) for i, b in enumerate(blocks[:-1])]
    last = len(blocks) - 1
    blocks += [top, bottom]
    pieces += [
        (last, 0, 2 * size),
        (last + 1, 0, half),
        (last, 2 * size + half, half),
        (last, 2 * size, half),
        (last + 2, 0, half),
    ]
    return blocks, pieces


def on_device(amplitudes, integrals, occupancy, tile_place):
    chips = NX * NZ
    per_chip = tile_place.shape[0] // chips
    rows, width = amplitudes.shape[2:]
    cols = integrals.shape[1]
    sent = pack(occupancy[0], tile_place, amplitudes[0], chips, per_chip)
    got = lax.all_to_all(sent, CHIPS, 0, 0, tiled=True)
    left = spread(got, rows, per_chip * width)
    blocks, pieces = gather_panel(integrals, left)
    early, depth = 0, 0
    while depth < EARLY * width:
        depth += pieces[early][2]
        early += 1
    part = product(left, 0, blocks, pieces[:early])
    part = product(left, depth, blocks, pieces[early:], part)
    part = part.reshape(NX, NZ * rows, cols)
    part = lax.all_to_all(part, "x", 0, 0, tiled=True).sum(axis=0)
    part = part.reshape(NZ, rows, cols)
    return lax.all_to_all(part, "z", 0, 0, tiled=True).sum(axis=0)


def solution(mesh):
    split_mesh = Mesh(mesh.devices.reshape(NX, NZ, NC, -1), EVERY)
    return jax.shard_map(
        on_device,
        mesh=split_mesh,
        in_specs=(
            P(EVERY, None, None, None),
            P(EVERY, None),
            P(EVERY, None),
            P(),
        ),
        out_specs=P(EVERY, None),
        check_vma=False,
    )
```

```python
import jax
import jax.numpy as jnp
from jax import lax
from jax.experimental import pallas as pl
from jax.experimental.pallas import tpu as pltpu
from jax.sharding import Mesh, PartitionSpec as P

NX, NZ, NC = 4, 8, 2
CAP = 4
CHIPS = ("x", "z")
EVERY = ("x", "z", "core", "grp")
LANES = 128
HEAD = 8
EARLY = 12
VMEM_LIMIT = 20 << 20
VMEM = pl.BlockSpec(memory_space=pltpu.VMEM)
SMEM = pl.BlockSpec(memory_space=pltpu.SMEM)
ANY = pl.BlockSpec(memory_space=pl.ANY)


def panel_position(core, grp, of_core, of_grp, n):
    ahead = jnp.where(core == 0, grp - of_grp + n, of_grp - grp + n) % n
    other = jnp.where(core == of_core, 0, 1)
    near = jnp.where(ahead == 0, 0, 4 * ahead - 2) + other
    back = 4 * (n - ahead) + 1 - other
    return jnp.where(ahead <= n // 2, near, back)


def pack_kernel(occ_ref, place_ref, amp_ref, out_ref, count_ref, where_ref):
    rows = amp_ref.shape[1]
    per_chip = where_ref.shape[0]
    per_core = per_chip // NC
    here = lax.axis_index("core"), lax.axis_index("grp")
    heading = jnp.full((HEAD, LANES), per_chip, jnp.int32).astype(jnp.float32)
    lane = lax.broadcasted_iota(jnp.int32, (HEAD, LANES), 1)

    def clear(i, carry):
        count_ref[i] = 0
        out_ref[i, pl.ds(0, HEAD), :] = heading
        return carry

    lax.fori_loop(0, count_ref.shape[0], clear, 0, unroll=4)
    for core in range(NC):
        for grp in range(per_core):
            where_ref[core * per_core + grp] = panel_position(*here, core, grp, per_core)

    def step(j, carry):
        place = place_ref[occ_ref[j]]
        chip = place // per_chip
        at = where_ref[place % per_chip]
        slot = count_ref[chip]
        count_ref[chip] = slot + 1
        out_ref[chip, pl.ds(pl.multiple_of(HEAD + slot * rows, 8), rows), :] = amp_ref[j]
        out_ref[chip, pl.ds(0, HEAD), :] = jnp.where(
            lane == slot, at.astype(jnp.float32), out_ref[chip, pl.ds(0, HEAD), :]
        )
        return carry

    lax.fori_loop(0, occ_ref.shape[0], step, 0, unroll=4)


def pack(occ, place, amp, chips, per_chip):
    rows, width = amp.shape[1:]
    return pl.pallas_call(
        pack_kernel,
        out_shape=jax.ShapeDtypeStruct((chips, HEAD + NC * CAP * rows, width), jnp.float32),
        in_specs=[SMEM, SMEM, VMEM],
        out_specs=VMEM,
        scratch_shapes=[pltpu.SMEM((chips,), jnp.int32), pltpu.SMEM((per_chip,), jnp.int32)],
        cost_estimate=pl.CostEstimate(flops=0, bytes_accessed=8 << 20, transcendentals=0),
        name="pack",
    )(occ, place, amp)


def split(value):
    high = value.astype(jnp.bfloat16)
    return high, (value - high.astype(jnp.float32)).astype(jnp.bfloat16)


def spread_kernel(got_ref, left_ref, head, sem):
    chips = got_ref.shape[0]
    height = left_ref.shape[0] // 2
    rows = height // chips
    copy = pltpu.make_async_copy(got_ref.at[:, pl.ds(0, HEAD), :], head, sem)
    copy.start()

    def clear(i, carry):
        at = pl.ds(pl.multiple_of(i * 32, 32), 32)
        left_ref[at, :] = jnp.zeros((32, left_ref.shape[1]), left_ref.dtype)
        return carry

    lax.fori_loop(0, left_ref.shape[0] // 32, clear, 0)
    copy.wait()

    def step(n, carry):
        row = pl.multiple_of(n * rows, rows)
        for s in range(NC * CAP):
            col = pl.multiple_of(head[n, 0, s].astype(jnp.int32) * LANES, LANES)
            high, low = split(got_ref[n, HEAD + s * rows : HEAD + (s + 1) * rows, :])
            left_ref[pl.ds(row, rows), pl.ds(col, LANES)] = high
            left_ref[pl.ds(height + row, rows), pl.ds(col, LANES)] = low
        return carry

    lax.fori_loop(0, chips, step, 0, unroll=2)


def spread(got, rows, depth):
    chips = got.shape[0]
    return pl.pallas_call(
        spread_kernel,
        out_shape=jax.ShapeDtypeStruct((2 * chips * rows, depth + LANES), jnp.bfloat16),
        in_specs=[VMEM],
        out_specs=VMEM,
        scratch_shapes=[
            pltpu.SMEM((chips, HEAD, LANES), jnp.float32),
            pltpu.SemaphoreType.DMA,
        ],
        cost_estimate=pl.CostEstimate(flops=0, bytes_accessed=8 << 20, transcendentals=0),
        compiler_params=pltpu.CompilerParams(vmem_limit_bytes=VMEM_LIMIT),
        name="spread",
    )(got)


def product_kernel(pieces, start, has_total, *refs):
    left_ref, refs = refs[0], refs[1:]
    if has_total:
        total_ref, refs = refs[0], refs[1:]
    panel, (out_ref, v_high, v_low) = refs[:-3], refs[-3:]
    height = out_ref.shape[0]
    depth = v_high.shape[0]
    at = 0
    for block, first, size in pieces:
        for i in range(0, size, 64):
            value = panel[block][first + i : first + i + 64, :]
            v_high[at : at + 64, :], v_low[at : at + 64, :] = split(value)
            at += 64
    dot = lambda a, b: jnp.dot(a, b, preferred_element_type=jnp.float32)
    wide = 256
    for i in range(0, out_ref.shape[1], wide):
        cols = pl.ds(i, wide)
        both = dot(left_ref[:, start : start + depth], v_high[:, cols])
        part = both[height:] + dot(left_ref[:height, start : start + depth], v_low[:, cols])
        part = both[:height] + part
        out_ref[:, cols] = part + total_ref[:, cols] if has_total else part


def product(left, start, blocks, pieces, total=None):
    height = left.shape[0] // 2
    depth = sum(size for _, _, size in pieces)
    cols = blocks[0].shape[1]
    used = sorted({piece[0] for piece in pieces})
    pieces = [(used.index(block), first, size) for block, first, size in pieces]
    extra = [] if total is None else [total]
    operands = [left] + extra + [blocks[i] for i in used]
    return pl.pallas_call(
        lambda *refs: product_kernel(pieces, start, bool(extra), *refs),
        out_shape=jax.ShapeDtypeStruct((height, cols), jnp.float32),
        in_specs=[VMEM] * len(operands),
        out_specs=VMEM,
        scratch_shapes=[
            pltpu.VMEM((depth, cols), jnp.bfloat16),
            pltpu.VMEM((depth, cols), jnp.bfloat16),
        ],
        cost_estimate=pl.CostEstimate(
            flops=6 * height * depth * cols, bytes_accessed=4 << 20, transcendentals=0
        ),
        compiler_params=pltpu.CompilerParams(vmem_limit_bytes=VMEM_LIMIT),
        name="product",
    )(*operands)


def swap_core(block):
    return lax.ppermute(block, "core", [(0, 1), (1, 0)])


def along_ring(block, cross=False):
    n = lax.axis_size("grp")
    up, down = (n, 0) if cross else (0, n)
    pairs = [(up + i, (i + 1) % n) for i in range(n)]
    pairs += [(down + i, n + (i - 1) % n) for i in range(n)]
    return lax.ppermute(block, ("core", "grp"), pairs)


def gather_panel(block, partner, own):
    n = lax.axis_size("grp")
    size = block.shape[0]
    mate = along_ring(block, cross=True)
    blocks = [block, partner, own, mate]
    for _ in range(n // 2 - 2):
        blocks.append(swap_core(jnp.concatenate([own, mate], axis=0)))
        own, mate = along_ring(own), along_ring(mate)
        blocks += [own, mate]
    far = along_ring(own)
    pieces = [(i, 0, each.shape[0]) for i, each in enumerate(blocks)]
    last = len(blocks)
    blocks += [swap_core(jnp.concatenate([own, mate, far], axis=0)), far]
    return blocks, pieces + [(last, 0, 2 * size), (last + 1, 0, size), (last, 2 * size, size)]


def on_device(amplitudes, integrals, occupancy, tile_place):
    chips = NX * NZ
    per_chip = tile_place.shape[0] // chips
    rows, width = amplitudes.shape[2:]
    cols = integrals.shape[1]
    sent = pack(occupancy[0], tile_place, amplitudes[0], chips, per_chip)
    sent, first, partner = lax.optimization_barrier(
        (sent, along_ring(integrals), swap_core(integrals))
    )
    got = lax.all_to_all(sent, CHIPS, 0, 0, tiled=True)
    blocks, pieces = gather_panel(integrals, partner, first)
    left = spread(got, rows, per_chip * width)
    early, depth = 0, 0
    while depth < EARLY * width:
        depth += pieces[early][2]
        early += 1
    part = product(left, 0, blocks, pieces[:early])
    part = product(left, depth, blocks, pieces[early:], part)
    part = part.reshape(NX, NZ * rows, cols)
    part = lax.all_to_all(part, "x", 0, 0, tiled=True).sum(axis=0)
    part = part.reshape(NZ, rows, cols)
    return lax.all_to_all(part, "z", 0, 0, tiled=True).sum(axis=0)


def solution(mesh):
    split_mesh = Mesh(mesh.devices.reshape(NX, NZ, NC, -1), EVERY)
    return jax.shard_map(
        on_device,
        mesh=split_mesh,
        in_specs=(
            P(EVERY, None, None, None),
            P(EVERY, None),
            P(EVERY, None),
            P(),
        ),
        out_specs=P(EVERY, None),
        check_vma=False,
    )
```

```python
import jax
import jax.numpy as jnp
from jax import lax
from jax.experimental import pallas as pl
from jax.experimental.pallas import tpu as pltpu
from jax.sharding import Mesh, PartitionSpec as P

NX, NZ, NC = 4, 8, 2
CAP = 4
CHIPS = ("x", "z")
EVERY = ("x", "z", "core", "grp")
LANES = 128
HEAD = 8
PRODUCT_LIMIT = 30 << 20
VMEM = pl.BlockSpec(memory_space=pltpu.VMEM)
SMEM = pl.BlockSpec(memory_space=pltpu.SMEM)
ANY = pl.BlockSpec(memory_space=pl.ANY)


def panel_position(core, grp, of_core, of_grp, n):
    ahead = jnp.where(core == 0, grp - of_grp + n, of_grp - grp + n) % n
    other = jnp.where(core == of_core, 0, 1)
    near = jnp.where(ahead == 0, 0, 4 * ahead - 2) + other
    back = 4 * (n - ahead) + 1 - other
    return jnp.where(ahead <= n // 2, near, back)


def pack_kernel(occ_ref, place_ref, amp_ref, out_ref, count_ref, where_ref):
    rows = amp_ref.shape[1]
    per_chip = where_ref.shape[0]
    per_core = per_chip // NC
    here = lax.axis_index("core"), lax.axis_index("grp")
    heading = jnp.full((HEAD, LANES), per_chip, jnp.int32).astype(jnp.float32)
    lane = lax.broadcasted_iota(jnp.int32, (HEAD, LANES), 1)

    def clear(i, carry):
        count_ref[i] = 0
        out_ref[i, pl.ds(0, HEAD), :] = heading
        return carry

    lax.fori_loop(0, count_ref.shape[0], clear, 0, unroll=4)
    for core in range(NC):
        for grp in range(per_core):
            where_ref[core * per_core + grp] = panel_position(*here, core, grp, per_core)

    def step(j, carry):
        place = place_ref[occ_ref[j]]
        chip = place // per_chip
        at = where_ref[place % per_chip]
        slot = count_ref[chip]
        count_ref[chip] = slot + 1
        out_ref[chip, pl.ds(pl.multiple_of(HEAD + slot * rows, 8), rows), :] = amp_ref[j]
        out_ref[chip, pl.ds(0, HEAD), :] = jnp.where(
            lane == slot, at.astype(jnp.float32), out_ref[chip, pl.ds(0, HEAD), :]
        )
        return carry

    lax.fori_loop(0, occ_ref.shape[0], step, 0, unroll=4)


def pack(occ, place, amp, chips, per_chip):
    rows, width = amp.shape[1:]
    return pl.pallas_call(
        pack_kernel,
        out_shape=jax.ShapeDtypeStruct((chips, HEAD + NC * CAP * rows, width), jnp.float32),
        in_specs=[SMEM, SMEM, VMEM],
        out_specs=VMEM,
        scratch_shapes=[pltpu.SMEM((chips,), jnp.int32), pltpu.SMEM((per_chip,), jnp.int32)],
        cost_estimate=pl.CostEstimate(flops=0, bytes_accessed=8 << 20, transcendentals=0),
        name="pack",
    )(occ, place, amp)


def split(value):
    high = value.astype(jnp.bfloat16)
    return high, (value - high.astype(jnp.float32)).astype(jnp.bfloat16)


def row_of(ahead, low, height):
    spot = (1 - low) if ahead % 2 else 2 + low
    return (((ahead + 3) % 4 // 2) * 4 + spot) * height


def spread_kernel(got_ref, left_ref, head, start, sem):
    chips = got_ref.shape[0]
    height = left_ref.shape[0] // (2 * NX)
    rows = height // NZ
    copy = pltpu.make_async_copy(got_ref.at[:, pl.ds(0, HEAD), :], head, sem)
    copy.start()
    here = lax.axis_index("x")
    for ahead in range(NX):
        for low in range(2):
            start[low, (here + ahead) % NX] = row_of(ahead, low, height)

    def clear(i, carry):
        at = pl.ds(pl.multiple_of(i * 32, 32), 32)
        left_ref[at, :] = jnp.zeros((32, left_ref.shape[1]), left_ref.dtype)
        return carry

    lax.fori_loop(0, left_ref.shape[0] // 32, clear, 0)
    copy.wait()

    def step(n, carry):
        row = (n % NZ) * rows
        high_row = pl.multiple_of(start[0, n // NZ] + row, rows)
        low_row = pl.multiple_of(start[1, n // NZ] + row, rows)
        for s in range(NC * CAP):
            col = pl.multiple_of(head[n, 0, s].astype(jnp.int32) * LANES, LANES)
            high, low = split(got_ref[n, HEAD + s * rows : HEAD + (s + 1) * rows, :])
            left_ref[pl.ds(high_row, rows), pl.ds(col, LANES)] = high
            left_ref[pl.ds(low_row, rows), pl.ds(col, LANES)] = low
        return carry

    lax.fori_loop(0, chips, step, 0, unroll=2)


def spread(got, rows, depth):
    chips = got.shape[0]
    return pl.pallas_call(
        spread_kernel,
        out_shape=jax.ShapeDtypeStruct((2 * chips * rows, depth + LANES), jnp.bfloat16),
        in_specs=[VMEM],
        out_specs=VMEM,
        scratch_shapes=[
            pltpu.SMEM((chips, HEAD, LANES), jnp.float32),
            pltpu.SMEM((2, NX), jnp.int32),
            pltpu.SemaphoreType.DMA,
        ],
        cost_estimate=pl.CostEstimate(flops=0, bytes_accessed=8 << 20, transcendentals=0),
        compiler_params=pltpu.CompilerParams(vmem_limit_bytes=20 << 20),
        name="spread",
    )(got)


def product_kernel(pair, pieces, *refs):
    left_ref, refs = refs[0], refs[1:]
    if pieces:
        panel, (first_ref, second_ref, v_high, v_low) = refs[:-4], refs[-4:]
        at = 0
        for block, start, size in pieces:
            for i in range(0, size, 64):
                value = panel[block][start + i : start + i + 64, :]
                v_high[at : at + 64, :], v_low[at : at + 64, :] = split(value)
                at += 64
    else:
        v_high, v_low, first_ref, second_ref = refs
    height = first_ref.shape[0]
    depth = v_high.shape[0]
    base = pair * 4 * height
    dot = lambda a, b: jnp.dot(a, b, preferred_element_type=jnp.float32)
    wide = 256
    for i in range(0, first_ref.shape[1], wide):
        cols = pl.ds(i, wide)
        four = dot(left_ref[base : base + 4 * height, :depth], v_high[:, cols])
        two = dot(left_ref[base + height : base + 3 * height, :depth], v_low[:, cols])
        first_ref[:, cols] = four[height : 2 * height] + (four[:height] + two[:height])
        second_ref[:, cols] = four[2 * height : 3 * height] + (four[3 * height :] + two[height:])


def product(left, pair, blocks, pieces=()):
    height = left.shape[0] // (2 * NX)
    cols = blocks[0].shape[1]
    depth = left.shape[1] - LANES
    part = jax.ShapeDtypeStruct((height, cols), jnp.float32)
    half = jax.ShapeDtypeStruct((depth, cols), jnp.bfloat16)
    outs = (part, part, half, half) if pieces else (part, part)
    return pl.pallas_call(
        lambda *refs: product_kernel(pair, pieces, *refs),
        out_shape=outs,
        in_specs=[VMEM] * (1 + len(blocks)),
        out_specs=(VMEM,) * len(outs),
        cost_estimate=pl.CostEstimate(
            flops=12 * height * depth * cols, bytes_accessed=4 << 20, transcendentals=0
        ),
        compiler_params=pltpu.CompilerParams(vmem_limit_bytes=PRODUCT_LIMIT),
        name="product",
    )(left, *blocks)


def shift_x(step):
    return [(i, (i + step) % NX) for i in range(NX)]


def swap_core(block):
    return lax.ppermute(block, "core", [(0, 1), (1, 0)])


def along_ring(block, cross=False):
    n = lax.axis_size("grp")
    up, down = (n, 0) if cross else (0, n)
    pairs = [(up + i, (i + 1) % n) for i in range(n)]
    pairs += [(down + i, n + (i - 1) % n) for i in range(n)]
    return lax.ppermute(block, ("core", "grp"), pairs)


def gather_panel(block, partner, own):
    n = lax.axis_size("grp")
    size = block.shape[0]
    mate = along_ring(block, cross=True)
    blocks = [block, partner, own, mate]
    for _ in range(n // 2 - 2):
        blocks.append(swap_core(jnp.concatenate([own, mate], axis=0)))
        own, mate = along_ring(own), along_ring(mate)
        blocks += [own, mate]
    far = along_ring(own)
    pieces = [(i, 0, each.shape[0]) for i, each in enumerate(blocks)]
    last = len(blocks)
    blocks += [swap_core(jnp.concatenate([own, mate, far], axis=0)), far]
    return blocks, pieces + [(last, 0, 2 * size), (last + 1, 0, size), (last, 2 * size, size)]


def on_device(amplitudes, integrals, occupancy, tile_place):
    chips = NX * NZ
    per_chip = tile_place.shape[0] // chips
    rows, width = amplitudes.shape[2:]
    cols = integrals.shape[1]
    sent = pack(occupancy[0], tile_place, amplitudes[0], chips, per_chip)
    sent, first, partner = lax.optimization_barrier(
        (sent, along_ring(integrals), swap_core(integrals))
    )
    got = lax.all_to_all(sent, CHIPS, 0, 0, tiled=True)
    blocks, pieces = gather_panel(integrals, partner, first)
    left = spread(got, rows, per_chip * width)
    near, far, high, low = product(left, 0, blocks, pieces)
    far = lax.ppermute(far, "x", shift_x(2))
    near = lax.ppermute(near, "x", shift_x(1))
    back, part = product(left, 1, [high, low])
    far, near, part = lax.optimization_barrier((far, near, part))
    back = lax.ppermute(back, "x", shift_x(-1))
    part = part + near + far + back
    part = part.reshape(NZ, rows, cols)
    return lax.all_to_all(part, "z", 0, 0, tiled=True).sum(axis=0)


def solution(mesh):
    split_mesh = Mesh(mesh.devices.reshape(NX, NZ, NC, -1), EVERY)
    return jax.shard_map(
        on_device,
        mesh=split_mesh,
        in_specs=(
            P(EVERY, None, None, None),
            P(EVERY, None),
            P(EVERY, None),
            P(),
        ),
        out_specs=P(EVERY, None),
        check_vma=False,
    )
```

```python
import jax
import jax.numpy as jnp
from jax import lax
from jax.experimental import pallas as pl
from jax.experimental.pallas import tpu as pltpu
from jax.sharding import Mesh, PartitionSpec as P

NX, NZ, NC = 4, 8, 2
CAP = 4
CHIPS = ("x", "z")
EVERY = ("x", "z", "core", "grp")
LANES = 128
HEAD = 8
PRODUCT_LIMIT = 30 << 20
VMEM = pl.BlockSpec(memory_space=pltpu.VMEM)
SMEM = pl.BlockSpec(memory_space=pltpu.SMEM)
ANY = pl.BlockSpec(memory_space=pl.ANY)


def panel_position(core, grp, of_core, of_grp, n):
    ahead = jnp.where(core == 0, grp - of_grp + n, of_grp - grp + n) % n
    other = jnp.where(core == of_core, 0, 1)
    near = jnp.where(ahead == 0, 0, 4 * ahead - 2) + other
    back = 4 * (n - ahead) + 1 - other
    return jnp.where(ahead <= n // 2, near, back)


def pack_kernel(occ_ref, place_ref, amp_ref, out_ref, count_ref, where_ref):
    rows = amp_ref.shape[1]
    per_chip = where_ref.shape[0]
    per_core = per_chip // NC
    here = lax.axis_index("core"), lax.axis_index("grp")
    heading = jnp.full((HEAD, LANES), per_chip, jnp.int32).astype(jnp.float32)
    lane = lax.broadcasted_iota(jnp.int32, (HEAD, LANES), 1)

    def clear(i, carry):
        count_ref[i] = 0
        out_ref[i, pl.ds(0, HEAD), :] = heading
        return carry

    lax.fori_loop(0, count_ref.shape[0], clear, 0, unroll=4)
    for core in range(NC):
        for grp in range(per_core):
            where_ref[core * per_core + grp] = panel_position(*here, core, grp, per_core)

    def step(j, carry):
        place = place_ref[occ_ref[j]]
        chip = place // per_chip
        at = where_ref[place % per_chip]
        slot = count_ref[chip]
        count_ref[chip] = slot + 1
        out_ref[chip, pl.ds(pl.multiple_of(HEAD + slot * rows, 8), rows), :] = amp_ref[j]
        out_ref[chip, pl.ds(0, HEAD), :] = jnp.where(
            lane == slot, at.astype(jnp.float32), out_ref[chip, pl.ds(0, HEAD), :]
        )
        return carry

    lax.fori_loop(0, occ_ref.shape[0], step, 0, unroll=4)


def pack(occ, place, amp, chips, per_chip):
    rows, width = amp.shape[1:]
    return pl.pallas_call(
        pack_kernel,
        out_shape=jax.ShapeDtypeStruct((chips, HEAD + NC * CAP * rows, width), jnp.float32),
        in_specs=[SMEM, SMEM, VMEM],
        out_specs=VMEM,
        scratch_shapes=[pltpu.SMEM((chips,), jnp.int32), pltpu.SMEM((per_chip,), jnp.int32)],
        cost_estimate=pl.CostEstimate(flops=0, bytes_accessed=8 << 20, transcendentals=0),
        name="pack",
    )(occ, place, amp)


def split(value):
    high = value.astype(jnp.bfloat16)
    return high, (value - high.astype(jnp.float32)).astype(jnp.bfloat16)


def row_of(ahead, low, height):
    spot = (1 - low) if ahead % 2 else 2 + low
    return (((ahead + 3) % 4 // 2) * 4 + spot) * height


def spread_kernel(got_ref, left_ref, head, start, sem):
    chips = got_ref.shape[0]
    height = left_ref.shape[0] // (2 * NX)
    rows = height // NZ
    copy = pltpu.make_async_copy(got_ref.at[:, pl.ds(0, HEAD), :], head, sem)
    copy.start()
    here = lax.axis_index("x")
    for ahead in range(NX):
        for low in range(2):
            start[low, (here + ahead) % NX] = row_of(ahead, low, height)

    def clear(i, carry):
        at = pl.ds(pl.multiple_of(i * 32, 32), 32)
        left_ref[at, :] = jnp.zeros((32, left_ref.shape[1]), left_ref.dtype)
        return carry

    lax.fori_loop(0, left_ref.shape[0] // 32, clear, 0)
    copy.wait()

    def step(n, carry):
        row = (n % NZ) * rows
        high_row = pl.multiple_of(start[0, n // NZ] + row, rows)
        low_row = pl.multiple_of(start[1, n // NZ] + row, rows)
        for s in range(NC * CAP):
            col = pl.multiple_of(head[n, 0, s].astype(jnp.int32) * LANES, LANES)
            high, low = split(got_ref[n, HEAD + s * rows : HEAD + (s + 1) * rows, :])
            left_ref[pl.ds(high_row, rows), pl.ds(col, LANES)] = high
            left_ref[pl.ds(low_row, rows), pl.ds(col, LANES)] = low
        return carry

    lax.fori_loop(0, chips, step, 0, unroll=2)


def spread(got, rows, depth):
    chips = got.shape[0]
    return pl.pallas_call(
        spread_kernel,
        out_shape=jax.ShapeDtypeStruct((2 * chips * rows, depth + LANES), jnp.bfloat16),
        in_specs=[VMEM],
        out_specs=VMEM,
        scratch_shapes=[
            pltpu.SMEM((chips, HEAD, LANES), jnp.float32),
            pltpu.SMEM((2, NX), jnp.int32),
            pltpu.SemaphoreType.DMA,
        ],
        cost_estimate=pl.CostEstimate(flops=0, bytes_accessed=8 << 20, transcendentals=0),
        compiler_params=pltpu.CompilerParams(vmem_limit_bytes=20 << 20),
        name="spread",
    )(got)


def product_kernel(pair, pieces, *refs):
    left_ref, refs = refs[0], refs[1:]
    if pieces:
        panel, (first_ref, second_ref, v_high, v_low) = refs[:-4], refs[-4:]
        at = 0
        for block, start, size in pieces:
            for i in range(0, size, 64):
                value = panel[block][start + i : start + i + 64, :]
                v_high[at : at + 64, :], v_low[at : at + 64, :] = split(value)
                at += 64
    else:
        v_high, v_low, first_ref, second_ref = refs
    height = first_ref.shape[0]
    depth = v_high.shape[0]
    base = pair * 4 * height
    dot = lambda a, b: jnp.dot(a, b, preferred_element_type=jnp.float32)
    wide = 256
    for i in range(0, first_ref.shape[1], wide):
        cols = pl.ds(i, wide)
        four = dot(left_ref[base : base + 4 * height, :depth], v_high[:, cols])
        two = dot(left_ref[base + height : base + 3 * height, :depth], v_low[:, cols])
        first_ref[:, cols] = four[height : 2 * height] + (four[:height] + two[:height])
        second_ref[:, cols] = four[2 * height : 3 * height] + (four[3 * height :] + two[height:])


def product(left, pair, blocks, pieces=()):
    height = left.shape[0] // (2 * NX)
    cols = blocks[0].shape[1]
    depth = left.shape[1] - LANES
    part = jax.ShapeDtypeStruct((height, cols), jnp.float32)
    half = jax.ShapeDtypeStruct((depth, cols), jnp.bfloat16)
    outs = (part, part, half, half) if pieces else (part, part)
    return pl.pallas_call(
        lambda *refs: product_kernel(pair, pieces, *refs),
        out_shape=outs,
        in_specs=[VMEM] * (1 + len(blocks)),
        out_specs=(VMEM,) * len(outs),
        cost_estimate=pl.CostEstimate(
            flops=12 * height * depth * cols, bytes_accessed=4 << 20, transcendentals=0
        ),
        compiler_params=pltpu.CompilerParams(vmem_limit_bytes=PRODUCT_LIMIT),
        name="product",
    )(left, *blocks)


def shift_x(step):
    return [(i, (i + step) % NX) for i in range(NX)]


def swap_core(block):
    return lax.ppermute(block, "core", [(0, 1), (1, 0)])


def along_ring(block, cross=False):
    n = lax.axis_size("grp")
    up, down = (n, 0) if cross else (0, n)
    pairs = [(up + i, (i + 1) % n) for i in range(n)]
    pairs += [(down + i, n + (i - 1) % n) for i in range(n)]
    return lax.ppermute(block, ("core", "grp"), pairs)


def gather_panel(block, partner, own):
    n = lax.axis_size("grp")
    size = block.shape[0]
    mate = along_ring(block, cross=True)
    blocks = [block, partner, own, mate]
    swaps = []
    for _ in range(n // 2 - 2):
        swaps.append(swap_core(jnp.concatenate([own, mate], axis=0)))
        own, mate = along_ring(own), along_ring(mate)
        blocks += [swaps[-1], own, mate]
    far = along_ring(own)
    held, *_ = lax.optimization_barrier((mate, swaps[0]))
    pieces = [(i, 0, each.shape[0]) for i, each in enumerate(blocks)]
    last = len(blocks)
    blocks += [swap_core(jnp.concatenate([own, held, far], axis=0)), far]
    return blocks, pieces + [(last, 0, 2 * size), (last + 1, 0, size), (last, 2 * size, size)]


def on_device(amplitudes, integrals, occupancy, tile_place):
    chips = NX * NZ
    per_chip = tile_place.shape[0] // chips
    rows, width = amplitudes.shape[2:]
    cols = integrals.shape[1]
    sent = pack(occupancy[0], tile_place, amplitudes[0], chips, per_chip)
    sent, first, partner = lax.optimization_barrier(
        (sent, along_ring(integrals), swap_core(integrals))
    )
    got = lax.all_to_all(sent, CHIPS, 0, 0, tiled=True)
    blocks, pieces = gather_panel(integrals, partner, first)
    left = spread(got, rows, per_chip * width)
    near, far, high, low = product(left, 0, blocks, pieces)
    far = lax.ppermute(far, "x", shift_x(2))
    near = lax.ppermute(near, "x", shift_x(1))
    back, part = product(left, 1, [high, low])
    far, near, part = lax.optimization_barrier((far, near, part))
    back = lax.ppermute(back, "x", shift_x(-1))
    part = part + near + far + back
    part = part.reshape(NZ, rows, cols)
    return lax.all_to_all(part, "z", 0, 0, tiled=True).sum(axis=0)


def solution(mesh):
    split_mesh = Mesh(mesh.devices.reshape(NX, NZ, NC, -1), EVERY)
    return jax.shard_map(
        on_device,
        mesh=split_mesh,
        in_specs=(
            P(EVERY, None, None, None),
            P(EVERY, None),
            P(EVERY, None),
            P(),
        ),
        out_specs=P(EVERY, None),
        check_vma=False,
    )
```

```python
import jax
import jax.numpy as jnp
from jax import lax
from jax.experimental import pallas as pl
from jax.experimental.pallas import tpu as pltpu
from jax.sharding import Mesh, PartitionSpec as P

NX, NZ, NC = 4, 8, 2
CAP = 4
CHIPS = ("x", "z")
EVERY = ("x", "z", "core", "grp")
LANES = 128
HEAD = 8
PRODUCT_LIMIT = 30 << 20
VMEM = pl.BlockSpec(memory_space=pltpu.VMEM)
SMEM = pl.BlockSpec(memory_space=pltpu.SMEM)
ANY = pl.BlockSpec(memory_space=pl.ANY)


def panel_position(core, grp, of_core, of_grp, n):
    ahead = jnp.where(core == 0, grp - of_grp + n, of_grp - grp + n) % n
    other = jnp.where(core == of_core, 0, 1)
    near = jnp.where(ahead == 0, 0, 4 * ahead - 2) + other
    back = 4 * (n - ahead) + 1 - other
    return jnp.where(ahead <= n // 2, near, back)


def pack_kernel(occ_ref, place_ref, amp_ref, out_ref, count_ref, where_ref):
    rows = amp_ref.shape[1]
    per_chip = where_ref.shape[0]
    per_core = per_chip // NC
    here = lax.axis_index("core"), lax.axis_index("grp")
    heading = jnp.full((HEAD, LANES), per_chip, jnp.int32).astype(jnp.float32)
    lane = lax.broadcasted_iota(jnp.int32, (HEAD, LANES), 1)

    def clear(i, carry):
        count_ref[i] = 0
        out_ref[i, pl.ds(0, HEAD), :] = heading
        return carry

    lax.fori_loop(0, count_ref.shape[0], clear, 0, unroll=4)
    for core in range(NC):
        for grp in range(per_core):
            where_ref[core * per_core + grp] = panel_position(*here, core, grp, per_core)

    def step(j, carry):
        place = place_ref[occ_ref[j]]
        chip = place // per_chip
        at = where_ref[place % per_chip]
        slot = count_ref[chip]
        count_ref[chip] = slot + 1
        out_ref[chip, pl.ds(pl.multiple_of(HEAD + slot * rows, 8), rows), :] = amp_ref[j]
        out_ref[chip, pl.ds(0, HEAD), :] = jnp.where(
            lane == slot, at.astype(jnp.float32), out_ref[chip, pl.ds(0, HEAD), :]
        )
        return carry

    lax.fori_loop(0, occ_ref.shape[0], step, 0, unroll=4)


def pack(occ, place, amp, chips, per_chip):
    rows, width = amp.shape[1:]
    return pl.pallas_call(
        pack_kernel,
        out_shape=jax.ShapeDtypeStruct((chips, HEAD + NC * CAP * rows, width), jnp.float32),
        in_specs=[SMEM, SMEM, VMEM],
        out_specs=VMEM,
        scratch_shapes=[pltpu.SMEM((chips,), jnp.int32), pltpu.SMEM((per_chip,), jnp.int32)],
        cost_estimate=pl.CostEstimate(flops=0, bytes_accessed=8 << 20, transcendentals=0),
        name="pack",
    )(occ, place, amp)


def split(value):
    high = value.astype(jnp.bfloat16)
    return high, (value - high.astype(jnp.float32)).astype(jnp.bfloat16)


def row_of(ahead, low, height):
    spot = (1 - low) if ahead % 2 else 2 + low
    return (((ahead + 3) % 4 // 2) * 4 + spot) * height


def spread_kernel(got_ref, left_ref, head, start, sem):
    chips = got_ref.shape[0]
    height = left_ref.shape[0] // (2 * NX)
    rows = height // NZ
    copy = pltpu.make_async_copy(got_ref.at[:, pl.ds(0, HEAD), :], head, sem)
    copy.start()
    here = lax.axis_index("x")
    for ahead in range(NX):
        for low in range(2):
            start[low, (here + ahead) % NX] = row_of(ahead, low, height)

    def clear(i, carry):
        at = pl.ds(pl.multiple_of(i * 32, 32), 32)
        left_ref[at, :] = jnp.zeros((32, left_ref.shape[1]), left_ref.dtype)
        return carry

    lax.fori_loop(0, left_ref.shape[0] // 32, clear, 0)
    copy.wait()

    def step(n, carry):
        row = (n % NZ) * rows
        high_row = pl.multiple_of(start[0, n // NZ] + row, rows)
        low_row = pl.multiple_of(start[1, n // NZ] + row, rows)
        for s in range(NC * CAP):
            col = pl.multiple_of(head[n, 0, s].astype(jnp.int32) * LANES, LANES)
            high, low = split(got_ref[n, HEAD + s * rows : HEAD + (s + 1) * rows, :])
            left_ref[pl.ds(high_row, rows), pl.ds(col, LANES)] = high
            left_ref[pl.ds(low_row, rows), pl.ds(col, LANES)] = low
        return carry

    lax.fori_loop(0, chips, step, 0, unroll=2)


def spread(got, rows, depth):
    chips = got.shape[0]
    return pl.pallas_call(
        spread_kernel,
        out_shape=jax.ShapeDtypeStruct((2 * chips * rows, depth + LANES), jnp.bfloat16),
        in_specs=[VMEM],
        out_specs=VMEM,
        scratch_shapes=[
            pltpu.SMEM((chips, HEAD, LANES), jnp.float32),
            pltpu.SMEM((2, NX), jnp.int32),
            pltpu.SemaphoreType.DMA,
        ],
        cost_estimate=pl.CostEstimate(flops=0, bytes_accessed=8 << 20, transcendentals=0),
        compiler_params=pltpu.CompilerParams(vmem_limit_bytes=20 << 20),
        name="spread",
    )(got)


def product_kernel(first, pieces, *refs):
    left_ref, panel = refs[0], refs[1 : -NX - 2]
    out_refs, (v_high, v_low) = refs[-NX - 2 : -2], refs[-2:]
    height, wide_cols = out_refs[0].shape
    depth = v_high.shape[0]
    at = 0
    for block, start, size in pieces:
        for i in range(0, size, 64):
            value = panel[block][start + i : start + i + 64, first : first + wide_cols]
            v_high[at : at + 64, :], v_low[at : at + 64, :] = split(value)
            at += 64
    dot = lambda a, b: jnp.dot(a, b, preferred_element_type=jnp.float32)
    wide = 256
    for i in range(0, wide_cols, wide):
        cols = pl.ds(i, wide)
        for pair in range(NX // 2):
            base = pair * 4 * height
            four = dot(left_ref[base : base + 4 * height, :depth], v_high[:, cols])
            two = dot(left_ref[base + height : base + 3 * height, :depth], v_low[:, cols])
            odd, even = 2 * pair + 1, (2 * pair + 2) % NX
            out_refs[odd][:, cols] = four[height : 2 * height] + (four[:height] + two[:height])
            out_refs[even][:, cols] = four[2 * height : 3 * height] + (
                four[3 * height :] + two[height:]
            )


def product(left, first, cols, blocks, pieces):
    height = left.shape[0] // (2 * NX)
    depth = left.shape[1] - LANES
    return pl.pallas_call(
        lambda *refs: product_kernel(first, pieces, *refs),
        out_shape=(jax.ShapeDtypeStruct((height, cols), jnp.float32),) * NX,
        in_specs=[VMEM] * (1 + len(blocks)),
        out_specs=(VMEM,) * NX,
        scratch_shapes=[
            pltpu.VMEM((depth, cols), jnp.bfloat16),
            pltpu.VMEM((depth, cols), jnp.bfloat16),
        ],
        cost_estimate=pl.CostEstimate(
            flops=6 * NX * height * depth * cols, bytes_accessed=4 << 20, transcendentals=0
        ),
        compiler_params=pltpu.CompilerParams(vmem_limit_bytes=PRODUCT_LIMIT),
        name="product",
    )(left, *blocks)


def shift_x(step):
    return [(i, (i + step) % NX) for i in range(NX)]


def swap_core(block):
    return lax.ppermute(block, "core", [(0, 1), (1, 0)])


def along_ring(block, cross=False):
    n = lax.axis_size("grp")
    up, down = (n, 0) if cross else (0, n)
    pairs = [(up + i, (i + 1) % n) for i in range(n)]
    pairs += [(down + i, n + (i - 1) % n) for i in range(n)]
    return lax.ppermute(block, ("core", "grp"), pairs)


def gather_panel(block, partner, own):
    n = lax.axis_size("grp")
    size = block.shape[0]
    mate = along_ring(block, cross=True)
    blocks = [block, partner, own, mate]
    swaps = []
    for _ in range(n // 2 - 2):
        swaps.append(swap_core(jnp.concatenate([own, mate], axis=0)))
        own, mate = along_ring(own), along_ring(mate)
        blocks += [swaps[-1], own, mate]
    far = along_ring(own)
    held, *_ = lax.optimization_barrier((mate, swaps[0]))
    held_far, *_ = lax.optimization_barrier((far, swaps[1]))
    pieces = [(i, 0, each.shape[0]) for i, each in enumerate(blocks)]
    last = len(blocks)
    blocks += [swap_core(jnp.concatenate([own, held, held_far], axis=0)), far]
    return blocks, pieces + [(last, 0, 2 * size), (last + 1, 0, size), (last, 2 * size, size)]


def on_device(amplitudes, integrals, occupancy, tile_place):
    chips = NX * NZ
    per_chip = tile_place.shape[0] // chips
    rows, width = amplitudes.shape[2:]
    cols = integrals.shape[1]
    sent = pack(occupancy[0], tile_place, amplitudes[0], chips, per_chip)
    sent, first, partner = lax.optimization_barrier(
        (sent, along_ring(integrals), swap_core(integrals))
    )
    got = lax.all_to_all(sent, CHIPS, 0, 0, tiled=True)
    blocks, pieces = gather_panel(integrals, partner, first)
    left = spread(got, rows, per_chip * width)
    wide = cols // 2
    send = lambda parts: [lax.ppermute(parts[i], "x", shift_x(i)) for i in (2, 1, 3)]
    one = product(left, 0, wide, blocks, pieces)
    got_one = send(one)
    two = product(left, wide, wide, blocks, pieces)
    got_one, held = lax.optimization_barrier((got_one, two[0]))
    got_two = send(two)
    over_z = lambda part: lax.all_to_all(
        part.reshape(NZ, rows, wide), "z", 0, 0, tiled=True
    )
    left_half = over_z(one[0] + got_one[0] + got_one[1] + got_one[2])
    got_two, left_half = lax.optimization_barrier((got_two, left_half))
    right_half = over_z(held + got_two[0] + got_two[1] + got_two[2])
    return jnp.concatenate([left_half.sum(axis=0), right_half.sum(axis=0)], axis=1)


def solution(mesh):
    split_mesh = Mesh(mesh.devices.reshape(NX, NZ, NC, -1), EVERY)
    return jax.shard_map(
        on_device,
        mesh=split_mesh,
        in_specs=(
            P(EVERY, None, None, None),
            P(EVERY, None),
            P(EVERY, None),
            P(),
        ),
        out_specs=P(EVERY, None),
        check_vma=False,
    )
```

```python
import jax
import jax.numpy as jnp
from jax import lax
from jax.experimental import pallas as pl
from jax.experimental.pallas import tpu as pltpu
from jax.sharding import Mesh, PartitionSpec as P

NX, NZ, NC = 4, 8, 2
CAP = 4
CHIPS = ("x", "z")
EVERY = ("x", "z", "core", "grp")
LANES = 128
HEAD = 8
PRODUCT_LIMIT = 30 << 20
VMEM = pl.BlockSpec(memory_space=pltpu.VMEM)
SMEM = pl.BlockSpec(memory_space=pltpu.SMEM)
ANY = pl.BlockSpec(memory_space=pl.ANY)


def panel_position(core, grp, of_core, of_grp, n):
    ahead = jnp.where(core == 0, grp - of_grp + n, of_grp - grp + n) % n
    other = jnp.where(core == of_core, 0, 1)
    near = jnp.where(ahead == 0, 0, 4 * ahead - 2) + other
    back = 4 * (n - ahead) + 1 - other
    return jnp.where(ahead <= n // 2, near, back)


def pack_kernel(occ_ref, place_ref, amp_ref, out_ref, count_ref, where_ref):
    rows = amp_ref.shape[1]
    per_chip = where_ref.shape[0]
    per_core = per_chip // NC
    here = lax.axis_index("core"), lax.axis_index("grp")
    heading = jnp.full((HEAD, LANES), per_chip, jnp.int32).astype(jnp.float32)
    lane = lax.broadcasted_iota(jnp.int32, (HEAD, LANES), 1)

    def clear(i, carry):
        count_ref[i] = 0
        out_ref[i, pl.ds(0, HEAD), :] = heading
        return carry

    lax.fori_loop(0, count_ref.shape[0], clear, 0, unroll=4)
    for core in range(NC):
        for grp in range(per_core):
            where_ref[core * per_core + grp] = panel_position(*here, core, grp, per_core)

    def step(j, carry):
        place = place_ref[occ_ref[j]]
        chip = place // per_chip
        at = where_ref[place % per_chip]
        slot = count_ref[chip]
        count_ref[chip] = slot + 1
        out_ref[chip, pl.ds(pl.multiple_of(HEAD + slot * rows, 8), rows), :] = amp_ref[j]
        out_ref[chip, pl.ds(0, HEAD), :] = jnp.where(
            lane == slot, at.astype(jnp.float32), out_ref[chip, pl.ds(0, HEAD), :]
        )
        return carry

    lax.fori_loop(0, occ_ref.shape[0], step, 0, unroll=4)


def pack(occ, place, amp, chips, per_chip):
    rows, width = amp.shape[1:]
    return pl.pallas_call(
        pack_kernel,
        out_shape=jax.ShapeDtypeStruct((chips, HEAD + NC * CAP * rows, width), jnp.float32),
        in_specs=[SMEM, SMEM, VMEM],
        out_specs=VMEM,
        scratch_shapes=[pltpu.SMEM((chips,), jnp.int32), pltpu.SMEM((per_chip,), jnp.int32)],
        cost_estimate=pl.CostEstimate(flops=0, bytes_accessed=8 << 20, transcendentals=0),
        name="pack",
    )(occ, place, amp)


def split(value):
    high = value.astype(jnp.bfloat16)
    return high, (value - high.astype(jnp.float32)).astype(jnp.bfloat16)


def row_of(ahead, low, height):
    spot = (1 - low) if ahead % 2 else 2 + low
    return (((ahead + 3) % 4 // 2) * 4 + spot) * height


def spread_kernel(got_ref, left_ref, head, start, sem):
    chips = got_ref.shape[0]
    height = left_ref.shape[0] // (2 * NX)
    rows = height // NZ
    copy = pltpu.make_async_copy(got_ref.at[:, pl.ds(0, HEAD), :], head, sem)
    copy.start()
    here = lax.axis_index("x")
    for ahead in range(NX):
        for low in range(2):
            start[low, (here + ahead) % NX] = row_of(ahead, low, height)

    def clear(i, carry):
        at = pl.ds(pl.multiple_of(i * 32, 32), 32)
        left_ref[at, :] = jnp.zeros((32, left_ref.shape[1]), left_ref.dtype)
        return carry

    lax.fori_loop(0, left_ref.shape[0] // 32, clear, 0)
    copy.wait()

    def step(n, carry):
        row = (n % NZ) * rows
        high_row = pl.multiple_of(start[0, n // NZ] + row, rows)
        low_row = pl.multiple_of(start[1, n // NZ] + row, rows)
        for s in range(NC * CAP):
            col = pl.multiple_of(head[n, 0, s].astype(jnp.int32) * LANES, LANES)
            high, low = split(got_ref[n, HEAD + s * rows : HEAD + (s + 1) * rows, :])
            left_ref[pl.ds(high_row, rows), pl.ds(col, LANES)] = high
            left_ref[pl.ds(low_row, rows), pl.ds(col, LANES)] = low
        return carry

    lax.fori_loop(0, chips, step, 0, unroll=2)


def spread(got, rows, depth):
    chips = got.shape[0]
    return pl.pallas_call(
        spread_kernel,
        out_shape=jax.ShapeDtypeStruct((2 * chips * rows, depth + LANES), jnp.bfloat16),
        in_specs=[VMEM],
        out_specs=VMEM,
        scratch_shapes=[
            pltpu.SMEM((chips, HEAD, LANES), jnp.float32),
            pltpu.SMEM((2, NX), jnp.int32),
            pltpu.SemaphoreType.DMA,
        ],
        cost_estimate=pl.CostEstimate(flops=0, bytes_accessed=8 << 20, transcendentals=0),
        compiler_params=pltpu.CompilerParams(vmem_limit_bytes=20 << 20),
        name="spread",
    )(got)


def product_kernel(pair, pieces, *refs):
    left_ref, refs = refs[0], refs[1:]
    if pieces:
        panel, (first_ref, second_ref, v_high, v_low) = refs[:-4], refs[-4:]
        at = 0
        for block, start, size in pieces:
            for i in range(0, size, 64):
                value = panel[block][start + i : start + i + 64, :]
                v_high[at : at + 64, :], v_low[at : at + 64, :] = split(value)
                at += 64
    else:
        v_high, v_low, first_ref, second_ref = refs
    height = first_ref.shape[0]
    depth = v_high.shape[0]
    base = pair * 4 * height
    dot = lambda a, b: jnp.dot(a, b, preferred_element_type=jnp.float32)
    wide = 256
    for i in range(0, first_ref.shape[1], wide):
        cols = pl.ds(i, wide)
        four = dot(left_ref[base : base + 4 * height, :depth], v_high[:, cols])
        two = dot(left_ref[base + height : base + 3 * height, :depth], v_low[:, cols])
        first_ref[:, cols] = four[height : 2 * height] + (four[:height] + two[:height])
        second_ref[:, cols] = four[2 * height : 3 * height] + (four[3 * height :] + two[height:])


def product(left, pair, blocks, pieces=()):
    height = left.shape[0] // (2 * NX)
    cols = blocks[0].shape[1]
    depth = left.shape[1] - LANES
    part = jax.ShapeDtypeStruct((height, cols), jnp.float32)
    half = jax.ShapeDtypeStruct((depth, cols), jnp.bfloat16)
    outs = (part, part, half, half) if pieces else (part, part)
    return pl.pallas_call(
        lambda *refs: product_kernel(pair, pieces, *refs),
        out_shape=outs,
        in_specs=[VMEM] * (1 + len(blocks)),
        out_specs=(VMEM,) * len(outs),
        cost_estimate=pl.CostEstimate(
            flops=12 * height * depth * cols, bytes_accessed=4 << 20, transcendentals=0
        ),
        compiler_params=pltpu.CompilerParams(vmem_limit_bytes=PRODUCT_LIMIT),
        name="product",
    )(left, *blocks)


def shift_x(step):
    return [(i, (i + step) % NX) for i in range(NX)]


def swap_core(block):
    return lax.ppermute(block, "core", [(0, 1), (1, 0)])


def along_ring(block, cross=False):
    n = lax.axis_size("grp")
    up, down = (n, 0) if cross else (0, n)
    pairs = [(up + i, (i + 1) % n) for i in range(n)]
    pairs += [(down + i, n + (i - 1) % n) for i in range(n)]
    return lax.ppermute(block, ("core", "grp"), pairs)


def gather_panel(block, partner, own):
    n = lax.axis_size("grp")
    size = block.shape[0]
    mate = along_ring(block, cross=True)
    blocks = [block, partner, own, mate]
    pairs = [(own, mate)]
    for _ in range(n // 2 - 2):
        own, mate = along_ring(own), along_ring(mate)
        pairs.append((own, mate))
    blocks = blocks[:2] + [each for pair in pairs for each in pair]
    early = [each for pair in pairs[:-1] for each in pair]
    swap = swap_core(jnp.concatenate(early, axis=0))
    far = along_ring(own)
    final = swap_core(jnp.concatenate([own, mate, far], axis=0))
    pieces = [(0, 0, size), (1, 0, size)]
    count = len(blocks)
    for i in range(len(pairs)):
        pieces += [(2 + 2 * i, 0, size), (3 + 2 * i, 0, size)]
        if i < len(pairs) - 1:
            pieces.append((count, 2 * i * size, 2 * size))
    blocks += [swap, final, far]
    pieces += [(count + 1, 0, 2 * size), (count + 2, 0, size), (count + 1, 2 * size, size)]
    return blocks, pieces


def on_device(amplitudes, integrals, occupancy, tile_place):
    chips = NX * NZ
    per_chip = tile_place.shape[0] // chips
    rows, width = amplitudes.shape[2:]
    cols = integrals.shape[1]
    sent = pack(occupancy[0], tile_place, amplitudes[0], chips, per_chip)
    sent, first, partner = lax.optimization_barrier(
        (sent, along_ring(integrals), swap_core(integrals))
    )
    got = lax.all_to_all(sent, CHIPS, 0, 0, tiled=True)
    blocks, pieces = gather_panel(integrals, partner, first)
    left = spread(got, rows, per_chip * width)
    near, far, high, low = product(left, 0, blocks, pieces)
    far = lax.ppermute(far, "x", shift_x(2))
    near = lax.ppermute(near, "x", shift_x(1))
    back, part = product(left, 1, [high, low])
    far, near, part = lax.optimization_barrier((far, near, part))
    back = lax.ppermute(back, "x", shift_x(-1))
    part = part + near + far + back
    part = part.reshape(NZ, rows, cols)
    return lax.all_to_all(part, "z", 0, 0, tiled=True).sum(axis=0)


def solution(mesh):
    split_mesh = Mesh(mesh.devices.reshape(NX, NZ, NC, -1), EVERY)
    return jax.shard_map(
        on_device,
        mesh=split_mesh,
        in_specs=(
            P(EVERY, None, None, None),
            P(EVERY, None),
            P(EVERY, None),
            P(),
        ),
        out_specs=P(EVERY, None),
        check_vma=False,
    )
```

```python
import jax
import jax.numpy as jnp
from jax import lax
from jax.experimental import pallas as pl
from jax.experimental.pallas import tpu as pltpu
from jax.sharding import Mesh, PartitionSpec as P

NX, NZ, NC = 4, 8, 2
CAP = 4
CHIPS = ("x", "z")
EVERY = ("x", "z", "core", "grp")
LANES = 128
HEAD = 8
PRODUCT_LIMIT = 30 << 20
VMEM = pl.BlockSpec(memory_space=pltpu.VMEM)
SMEM = pl.BlockSpec(memory_space=pltpu.SMEM)
ANY = pl.BlockSpec(memory_space=pl.ANY)


def panel_position(core, grp, of_core, of_grp, n):
    ahead = jnp.where(core == 0, grp - of_grp + n, of_grp - grp + n) % n
    other = jnp.where(core == of_core, 0, 1)
    near = jnp.where(ahead == 0, 0, 4 * ahead - 2) + other
    back = 4 * (n - ahead) + 1 - other
    return jnp.where(ahead <= n // 2, near, back)


def pack_kernel(occ_ref, place_ref, amp_ref, out_ref, count_ref, where_ref):
    rows = amp_ref.shape[1]
    per_chip = where_ref.shape[0]
    per_core = per_chip // NC
    here = lax.axis_index("core"), lax.axis_index("grp")
    heading = jnp.full((HEAD, LANES), per_chip, jnp.int32).astype(jnp.float32)
    lane = lax.broadcasted_iota(jnp.int32, (HEAD, LANES), 1)

    def clear(i, carry):
        count_ref[i] = 0
        out_ref[i, pl.ds(0, HEAD), :] = heading
        return carry

    lax.fori_loop(0, count_ref.shape[0], clear, 0, unroll=4)
    for core in range(NC):
        for grp in range(per_core):
            where_ref[core * per_core + grp] = panel_position(*here, core, grp, per_core)

    def step(j, carry):
        place = place_ref[occ_ref[j]]
        chip = place // per_chip
        at = where_ref[place % per_chip]
        slot = count_ref[chip]
        count_ref[chip] = slot + 1
        out_ref[chip, pl.ds(pl.multiple_of(HEAD + slot * rows, 8), rows), :] = amp_ref[j]
        out_ref[chip, pl.ds(0, HEAD), :] = jnp.where(
            lane == slot, at.astype(jnp.float32), out_ref[chip, pl.ds(0, HEAD), :]
        )
        return carry

    lax.fori_loop(0, occ_ref.shape[0], step, 0, unroll=4)


def pack(occ, place, amp, chips, per_chip):
    rows, width = amp.shape[1:]
    return pl.pallas_call(
        pack_kernel,
        out_shape=jax.ShapeDtypeStruct((chips, HEAD + NC * CAP * rows, width), jnp.float32),
        in_specs=[SMEM, SMEM, VMEM],
        out_specs=VMEM,
        scratch_shapes=[pltpu.SMEM((chips,), jnp.int32), pltpu.SMEM((per_chip,), jnp.int32)],
        cost_estimate=pl.CostEstimate(flops=0, bytes_accessed=8 << 20, transcendentals=0),
        name="pack",
    )(occ, place, amp)


def split(value):
    high = value.astype(jnp.bfloat16)
    return high, (value - high.astype(jnp.float32)).astype(jnp.bfloat16)


def row_of(ahead, low, height):
    spot = (1 - low) if ahead % 2 else 2 + low
    return (((ahead + 3) % 4 // 2) * 4 + spot) * height


def spread_kernel(got_ref, left_ref, head, start, sem):
    chips = got_ref.shape[0]
    height = left_ref.shape[0] // (2 * NX)
    rows = height // NZ
    copy = pltpu.make_async_copy(got_ref.at[:, pl.ds(0, HEAD), :], head, sem)
    copy.start()
    here = lax.axis_index("x")
    for ahead in range(NX):
        for low in range(2):
            start[low, (here + ahead) % NX] = row_of(ahead, low, height)

    def clear(i, carry):
        at = pl.ds(pl.multiple_of(i * 32, 32), 32)
        left_ref[at, :] = jnp.zeros((32, left_ref.shape[1]), left_ref.dtype)
        return carry

    lax.fori_loop(0, left_ref.shape[0] // 32, clear, 0)
    copy.wait()

    def step(n, carry):
        row = (n % NZ) * rows
        high_row = pl.multiple_of(start[0, n // NZ] + row, rows)
        low_row = pl.multiple_of(start[1, n // NZ] + row, rows)
        for s in range(NC * CAP):
            col = pl.multiple_of(head[n, 0, s].astype(jnp.int32) * LANES, LANES)
            high, low = split(got_ref[n, HEAD + s * rows : HEAD + (s + 1) * rows, :])
            left_ref[pl.ds(high_row, rows), pl.ds(col, LANES)] = high
            left_ref[pl.ds(low_row, rows), pl.ds(col, LANES)] = low
        return carry

    lax.fori_loop(0, chips, step, 0, unroll=2)


def spread(got, rows, depth):
    chips = got.shape[0]
    return pl.pallas_call(
        spread_kernel,
        out_shape=jax.ShapeDtypeStruct((2 * chips * rows, depth + LANES), jnp.bfloat16),
        in_specs=[VMEM],
        out_specs=VMEM,
        scratch_shapes=[
            pltpu.SMEM((chips, HEAD, LANES), jnp.float32),
            pltpu.SMEM((2, NX), jnp.int32),
            pltpu.SemaphoreType.DMA,
        ],
        cost_estimate=pl.CostEstimate(flops=0, bytes_accessed=8 << 20, transcendentals=0),
        compiler_params=pltpu.CompilerParams(vmem_limit_bytes=20 << 20),
        name="spread",
    )(got)


def product_kernel(pair, pieces, *refs):
    left_ref, refs = refs[0], refs[1:]
    if pieces:
        panel, (first_ref, second_ref, v_high, v_low) = refs[:-4], refs[-4:]
        at = 0
        for block, start, size in pieces:
            for i in range(0, size, 64):
                value = panel[block][start + i : start + i + 64, :]
                v_high[at : at + 64, :], v_low[at : at + 64, :] = split(value)
                at += 64
    else:
        v_high, v_low, first_ref, second_ref = refs
    height = first_ref.shape[0]
    depth = v_high.shape[0]
    base = pair * 4 * height
    dot = lambda a, b: jnp.dot(a, b, preferred_element_type=jnp.float32)
    wide = 256
    for i in range(0, first_ref.shape[1], wide):
        cols = pl.ds(i, wide)
        four = dot(left_ref[base : base + 4 * height, :depth], v_high[:, cols])
        two = dot(left_ref[base + height : base + 3 * height, :depth], v_low[:, cols])
        first_ref[:, cols] = four[height : 2 * height] + (four[:height] + two[:height])
        second_ref[:, cols] = four[2 * height : 3 * height] + (four[3 * height :] + two[height:])


def product(left, pair, blocks, pieces=()):
    height = left.shape[0] // (2 * NX)
    cols = blocks[0].shape[1]
    depth = left.shape[1] - LANES
    part = jax.ShapeDtypeStruct((height, cols), jnp.float32)
    half = jax.ShapeDtypeStruct((depth, cols), jnp.bfloat16)
    outs = (part, part, half, half) if pieces else (part, part)
    return pl.pallas_call(
        lambda *refs: product_kernel(pair, pieces, *refs),
        out_shape=outs,
        in_specs=[VMEM] * (1 + len(blocks)),
        out_specs=(VMEM,) * len(outs),
        cost_estimate=pl.CostEstimate(
            flops=12 * height * depth * cols, bytes_accessed=4 << 20, transcendentals=0
        ),
        compiler_params=pltpu.CompilerParams(vmem_limit_bytes=PRODUCT_LIMIT),
        name="product",
    )(left, *blocks)


def shift_x(step):
    return [(i, (i + step) % NX) for i in range(NX)]


def swap_core(block):
    return lax.ppermute(block, "core", [(0, 1), (1, 0)])


def along_ring(block, cross=False):
    n = lax.axis_size("grp")
    up, down = (n, 0) if cross else (0, n)
    pairs = [(up + i, (i + 1) % n) for i in range(n)]
    pairs += [(down + i, n + (i - 1) % n) for i in range(n)]
    return lax.ppermute(block, ("core", "grp"), pairs)


def gather_panel(block, partner, own):
    n = lax.axis_size("grp")
    size = block.shape[0]
    mate = along_ring(block, cross=True)
    blocks = [block, partner, own, mate]
    pairs = [(own, mate)]
    for _ in range(n // 2 - 2):
        own, mate = along_ring(own), along_ring(mate)
        pairs.append((own, mate))
    blocks = blocks[:2] + [each for pair in pairs for each in pair]
    early = [each for pair in pairs[:-1] for each in pair]
    swap = swap_core(jnp.concatenate(early, axis=0))
    far = along_ring(own)
    final = swap_core(jnp.concatenate([own, mate, far], axis=0))
    pieces = [(0, 0, size), (1, 0, size)]
    count = len(blocks)
    for i in range(len(pairs)):
        pieces += [(2 + 2 * i, 0, size), (3 + 2 * i, 0, size)]
        if i < len(pairs) - 1:
            pieces.append((count, 2 * i * size, 2 * size))
    blocks += [swap, final, far]
    pieces += [(count + 1, 0, 2 * size), (count + 2, 0, size), (count + 1, 2 * size, size)]
    return blocks, pieces


def on_device(amplitudes, integrals, occupancy, tile_place):
    chips = NX * NZ
    per_chip = tile_place.shape[0] // chips
    rows, width = amplitudes.shape[2:]
    cols = integrals.shape[1]
    sent = pack(occupancy[0], tile_place, amplitudes[0], chips, per_chip)
    first, partner = along_ring(integrals), swap_core(integrals)
    got = lax.all_to_all(sent, CHIPS, 0, 0, tiled=True)
    blocks, pieces = gather_panel(integrals, partner, first)
    left = spread(got, rows, per_chip * width)
    near, far, high, low = product(left, 0, blocks, pieces)
    far = lax.ppermute(far, "x", shift_x(2))
    near = lax.ppermute(near, "x", shift_x(1))
    back, part = product(left, 1, [high, low])
    far, near, part = lax.optimization_barrier((far, near, part))
    back = lax.ppermute(back, "x", shift_x(-1))
    part = part + near + far + back
    part = part.reshape(NZ, rows, cols)
    return lax.all_to_all(part, "z", 0, 0, tiled=True).sum(axis=0)


def solution(mesh):
    split_mesh = Mesh(mesh.devices.reshape(NX, NZ, NC, -1), EVERY)
    return jax.shard_map(
        on_device,
        mesh=split_mesh,
        in_specs=(
            P(EVERY, None, None, None),
            P(EVERY, None),
            P(EVERY, None),
            P(),
        ),
        out_specs=P(EVERY, None),
        check_vma=False,
    )
```
